32 devices in a mesh: groups: 2 (over y), seq: 4 (over z), head: 2 (over x), dp: 2 (over core).
Axes of the slice: x: 2, y: 2, z: 4, core: 2. Of those that a mesh axis runs over, the one named last changes fastest.
Arguments:
- x_input: bfloat16 [4, 1024, 5120], P(('groups', 'dp'), 'seq', 'head'), parts along dimension 0, may hold values from -6 to 6
- bc_input: bfloat16 [4, 1024, 256], P(('groups', 'dp'), 'seq'), parts along dimension 0, may hold values from -6 to 6
- decays: float32 [4, 80, 1024], P(('groups', 'dp'), 'head', 'seq'), parts along dimension 0, may hold values from 0.5 to 1, as said below
- conv_x: float32 [4, 5120], P(None, 'head'), may hold values from -3 to 3
- conv_bc: float32 [4, 256], replicated, may hold values from -3 to 3
- skip_gain: float32 [80], P('head'), may hold values from 0.5 to 2
- grad_out: bfloat16 [4, 1024, 5120], P(('groups', 'dp'), 'seq', 'head'), parts along dimension 0, may hold values from -6 to 6
Outputs:
- y_output: bfloat16 [4, 1024, 5120], P(('groups', 'dp'), 'seq', 'head'), parts along dimension 0
- grad_x: bfloat16 [4, 1024, 5120], P(('groups', 'dp'), 'seq', 'head'), parts along dimension 0
- grad_bc: bfloat16 [4, 1024, 256], P(('groups', 'dp'), 'seq'), parts along dimension 0
- grad_conv_x: float32 [8, 5120], P('groups', 'head'), parts along dimension 0
- grad_conv_bc: float32 [8, 256], P('groups'), parts along dimension 0
- grad_skip: float32 [160], P(('groups', 'head')), parts along dimension 0
The draws below stay inside these ranges and needn't reach their ends.
There are 2 independent parts, one for each index of `groups`. The reference program is written for one: setup_inputs(seed, part) draws one part's arguments, and reference() takes and returns one part's arrays. A program takes and returns all parts, laid end to end along the dimension named above; an argument that names none is the same for every part. Nothing has to cross between parts.
Inputs may be any that keep to these rules, and one draw needn't show every extreme that they name: `decays`: every decay is strictly below 1.
All inputs are finite; a program needn't handle non-finite values.
Results may differ from the reference program's by a relative error of at most 0.009.
Values may be sent and summed in bfloat16 or wider, within the bound.
A program may use at most 64 MiB of HBM per device.

```python
import math
import jax
import jax.numpy as jnp
from jax import lax

NUMBER_OF_HEADS = 80
HEAD_DIM = 64
STATE_DIM = 128
BLOCK_LEN = 256
CONV_WIDTH = 4
INNER_DIM = 5120
SEQUENCE_LENGTH = 1024
GROUP_SEQUENCES = 2


def draw_decays(key, part):
    random_subkeys = jax.random.split(key, 7)
    position = jnp.arange(SEQUENCE_LENGTH, dtype=jnp.float32)[None, None, :]
    fast_share = 0.5
    head_shape = (GROUP_SEQUENCES, NUMBER_OF_HEADS, 1)
    full_shape = (GROUP_SEQUENCES, NUMBER_OF_HEADS, SEQUENCE_LENGTH)
    is_fast = jax.random.uniform(random_subkeys[0], head_shape) < fast_share
    memory = jnp.exp(jax.random.uniform(random_subkeys[1], head_shape, minval=math.log(30.0), maxval=math.log(50.0)))
    slow_rate = jnp.exp(jax.random.uniform(random_subkeys[2], head_shape, minval=math.log(0.05), maxval=math.log(0.6))) / SEQUENCE_LENGTH
    base_rate = jnp.where(is_fast, 1.0 / memory, slow_rate)
    jitter = jnp.exp(jax.random.uniform(random_subkeys[3], full_shape, minval=-0.7, maxval=0.7))
    phase_shift = jax.random.uniform(random_subkeys[4], head_shape, minval=0.0, maxval=2.0 * math.pi)
    wave_factor = jnp.exp(0.7 * jnp.sin(2.0 * math.pi * 3.0 * position / SEQUENCE_LENGTH + phase_shift))
    every_rate = base_rate * jitter * wave_factor
    spike_position = jax.random.randint(random_subkeys[5], (GROUP_SEQUENCES, NUMBER_OF_HEADS, 2), 0, SEQUENCE_LENGTH)
    spike_flag = jnp.any(jnp.arange(SEQUENCE_LENGTH)[None, None, :, None] == spike_position[:, :, None, :], axis=-1)
    retained_values = jax.random.uniform(random_subkeys[6], full_shape, minval=0.5, maxval=0.8)
    logarithm_decay = jnp.where(spike_flag, jnp.log(retained_values), -every_rate)
    return jnp.exp(logarithm_decay).astype(jnp.float32)


def block_scale(own_key, shape, shards, least, top_value):
    gain, own = 1.0, jax.random.fold_in(own_key, 6)
    for axis_at, parts in shards:
        heights = jnp.exp(jax.random.uniform(jax.random.fold_in(own, axis_at), (parts,), jnp.float32, least / len(shards), top_value / len(shards)))
        gain = gain * jnp.repeat(heights, shape[axis_at] // parts).reshape([-1 if axis == axis_at else 1 for axis in range(len(shape))])
    return gain


def normal_values(key, shape, width, most, cuts=(), held_as=jnp.bfloat16):
    level = block_scale(key, shape, cuts, -0.22, 0.18) if cuts else 1.0
    array = jax.random.normal(key, shape, jnp.float32) * width * level
    return jnp.minimum(jnp.maximum(array, -most), most).astype(held_as)


def setup_inputs(seed: int = 0, part: int = 0) -> dict:
    splits = jax.random.split(jax.random.key(seed), 8)
    part_keys = jax.random.split(jax.random.fold_in(splits[7], part), 8)
    return {
        "x_input": normal_values(part_keys[0], (GROUP_SEQUENCES, SEQUENCE_LENGTH, INNER_DIM), 1.0, 6.0, ((0, 2), (1, 4), (2, 2))),
        "bc_input": normal_values(part_keys[1], (GROUP_SEQUENCES, SEQUENCE_LENGTH, 2 * STATE_DIM), 1.0, 6.0, ((0, 2), (1, 4))),
        "decays": draw_decays(jax.random.fold_in(jax.random.fold_in(splits[7], part), 71), part),
        "conv_x": normal_values(splits[3], (CONV_WIDTH, INNER_DIM), CONV_WIDTH ** -0.5, 3.0, ((1, 2),), jnp.float32),
        "conv_bc": normal_values(splits[4], (CONV_WIDTH, 2 * STATE_DIM), CONV_WIDTH ** -0.5, 3.0, (), jnp.float32),
        "skip_gain": jnp.clip(jnp.exp(math.log(2.0) - 1.3862944 * jax.random.uniform(splits[5], (NUMBER_OF_HEADS,), jnp.float32) ** block_scale(splits[5], (NUMBER_OF_HEADS,), ((0, 2),), -0.2, 0.2)), 0.5, 2.0),
        "grad_out": normal_values(part_keys[6], (GROUP_SEQUENCES, SEQUENCE_LENGTH, INNER_DIM), 1.0, 6.0, ((0, 2), (1, 4), (2, 2))),
    }


highest = lax.Precision.HIGHEST

def silu_grad(pre):
    sigma = jax.nn.sigmoid(pre)
    return sigma * (1.0 + pre * (1.0 - sigma))

def conv_forward(padded, weight, length):
    total = jnp.zeros((length, weight.shape[1]), jnp.float32)
    for shift in range(weight.shape[0]):
        total = total + weight[shift][None, :] * padded[shift:shift + length].astype(jnp.float32)
    return total

def conv_backward(pregrad, weight):
    taps = weight.shape[0]
    length = pregrad.shape[0]
    padded = jnp.concatenate([pregrad, jnp.zeros((taps - 1, pregrad.shape[1]), jnp.float32)], axis=0)
    total = jnp.zeros(pregrad.shape, jnp.float32)
    for shift in range(taps):
        total = total + weight[shift][None, :] * padded[taps - 1 - shift:taps - 1 - shift + length]
    return total

def conv_weight_grad(pregrad, padded, taps):
    length = pregrad.shape[0]
    return jnp.stack([lax.optimization_barrier(jnp.sum(pregrad * padded[shift:shift + length].astype(jnp.float32), axis=0)) for shift in range(taps)])

def decay_matrix(cum_block):
    size = cum_block.shape[-1]
    rows = jnp.arange(size)
    lower = (rows[:, None] >= rows[None, :])[None]
    diff = cum_block[:, :, None] - cum_block[:, None, :]
    return jnp.where(lower, jnp.exp(jnp.where(lower, diff, 0.0)), 0.0)

def one_row(x_row, bc_row, decay_row, conv_x, conv_bc, skip_gain, grad_row):
    length = x_row.shape[0]
    scale = STATE_DIM ** (-0.5)
    taps = CONV_WIDTH
    x_pad = jnp.concatenate([jnp.zeros((taps - 1, INNER_DIM), jnp.bfloat16), x_row], axis=0)
    bc_pad = jnp.concatenate([jnp.zeros((taps - 1, 2 * STATE_DIM), jnp.bfloat16), bc_row], axis=0)
    pre_x = conv_forward(x_pad, conv_x, length)
    pre_bc = conv_forward(bc_pad, conv_bc, length)
    inner = jax.nn.silu(pre_x).astype(jnp.bfloat16)
    mapped = jax.nn.silu(pre_bc).astype(jnp.bfloat16)
    b_mat = mapped[:, :STATE_DIM]
    c_mat = mapped[:, STATE_DIM:]
    logarithm_decay = jnp.log(decay_row)
    input_gain = jnp.sqrt(-jnp.expm1(2.0 * logarithm_decay))
    inner_heads = inner.astype(jnp.float32).reshape(length, NUMBER_OF_HEADS, HEAD_DIM)
    weighted = (inner_heads * input_gain.T[:, :, None]).astype(jnp.bfloat16)
    blocks = length // BLOCK_LEN
    cum = jnp.cumsum(logarithm_decay.reshape(NUMBER_OF_HEADS, blocks, BLOCK_LEN), axis=-1).transpose(1, 0, 2)
    w_blocks = weighted.reshape(blocks, BLOCK_LEN, NUMBER_OF_HEADS, HEAD_DIM)
    b_blocks = b_mat.reshape(blocks, BLOCK_LEN, STATE_DIM)
    c_blocks = c_mat.reshape(blocks, BLOCK_LEN, STATE_DIM)
    g_blocks = grad_row.reshape(blocks, BLOCK_LEN, NUMBER_OF_HEADS, HEAD_DIM)

    def forward_step(state, item):
        cum_b, w_b, b_b, c_b = item
        sim = jnp.dot(c_b, b_b.T, preferred_element_type=jnp.float32)
        mixing = (decay_matrix(cum_b) * sim[None]).astype(jnp.bfloat16)
        intra = jnp.einsum('hij,jhp->ihp', mixing.astype(jnp.float32), w_b.astype(jnp.float32))
        inter = jnp.exp(cum_b).T[:, :, None] * jnp.einsum('in,hpn->ihp', c_b.astype(jnp.float32), state, precision=highest)
        tail = jnp.exp(cum_b[:, -1:] - cum_b)
        update = jnp.einsum('jhp,jn->hpn', w_b.astype(jnp.float32) * tail.T[:, :, None], b_b.astype(jnp.float32), precision=highest)
        return (jnp.exp(cum_b[:, -1])[:, None, None] * state + update, (intra + inter, state))
    zero_state = jnp.zeros((NUMBER_OF_HEADS, HEAD_DIM, STATE_DIM), jnp.float32)
    final_state, (mixed, prior) = lax.scan(forward_step, zero_state, (cum, w_blocks, b_blocks, c_blocks))
    skip_rep = jnp.repeat(skip_gain, HEAD_DIM)[None, :]
    y_row = (scale * mixed.reshape(length, INNER_DIM) + skip_rep * inner.astype(jnp.float32)).astype(jnp.bfloat16)

    def backward_step(grad, item):
        cum_b, w_b, b_b, c_b, g_b, prior_b = item
        sim = jnp.dot(c_b, b_b.T, preferred_element_type=jnp.float32)
        decay_b = decay_matrix(cum_b)
        mixing = (decay_b * sim[None]).astype(jnp.bfloat16)
        g_f = g_b.astype(jnp.float32)
        w_f = w_b.astype(jnp.float32)
        tail = jnp.exp(cum_b[:, -1:] - cum_b)
        d_w = scale * jnp.einsum('hij,ihp->jhp', mixing.astype(jnp.float32), g_f)
        d_w = d_w + tail.T[:, :, None] * jnp.einsum('jn,hpn->jhp', b_b.astype(jnp.float32), grad, precision=highest)
        d_mix = scale * jnp.einsum('ihp,jhp->hij', g_f, w_f)
        d_sim = lax.optimization_barrier(jnp.sum(d_mix * decay_b, axis=0))
        lead = scale * g_f * jnp.exp(cum_b).T[:, :, None]
        d_c = jnp.dot(d_sim, b_b.astype(jnp.float32), precision=highest)
        d_c = d_c + jnp.einsum('ihp,hpn->in', lead, prior_b, precision=highest)
        d_b = jnp.dot(d_sim.T, c_b.astype(jnp.float32), precision=highest)
        d_b = d_b + jnp.einsum('jhp,hpn->jn', w_f * tail.T[:, :, None], grad, precision=highest)
        new_grad = jnp.exp(cum_b[:, -1])[:, None, None] * grad + jnp.einsum('ihp,in->hpn', lead, c_b.astype(jnp.float32), precision=highest)
        return (new_grad, (d_w, d_b, d_c))
    start_grad, (d_weighted, d_bmat, d_cmat) = lax.scan(backward_step, zero_state, (cum, w_blocks, b_blocks, c_blocks, g_blocks, prior), reverse=True)
    d_weighted = d_weighted.reshape(length, NUMBER_OF_HEADS, HEAD_DIM)
    d_inner = (input_gain.T[:, :, None] * d_weighted).reshape(length, INNER_DIM) + skip_rep * grad_row.astype(jnp.float32)
    d_pre_x = d_inner * silu_grad(pre_x)
    d_mapped = jnp.concatenate([d_bmat.reshape(length, STATE_DIM), d_cmat.reshape(length, STATE_DIM)], axis=1)
    d_pre_bc = d_mapped * silu_grad(pre_bc)
    grad_x = conv_backward(d_pre_x, conv_x).astype(jnp.bfloat16)
    grad_bc = conv_backward(d_pre_bc, conv_bc).astype(jnp.bfloat16)
    taps_x = conv_weight_grad(d_pre_x, x_pad, taps)
    taps_bc = conv_weight_grad(d_pre_bc, bc_pad, taps)
    skip_term = lax.optimization_barrier(jnp.sum((grad_row.astype(jnp.float32) * inner.astype(jnp.float32)).reshape(length, NUMBER_OF_HEADS, HEAD_DIM), axis=(0, 2)))
    return (y_row, grad_x, grad_bc, taps_x, taps_bc, skip_term)

def reference(x_input, bc_input, decays, conv_x, conv_bc, skip_gain, grad_out):
    outputs = [one_row(x_input[row], bc_input[row], decays[row], conv_x, conv_bc, skip_gain, grad_out[row]) for row in range(GROUP_SEQUENCES)]
    y_output = jnp.stack([item[0] for item in outputs])
    grad_x = jnp.stack([item[1] for item in outputs])
    grad_bc = jnp.stack([item[2] for item in outputs])
    norm_tokens = float(GROUP_SEQUENCES * SEQUENCE_LENGTH) ** (-0.5)
    norm_skip = float(GROUP_SEQUENCES * SEQUENCE_LENGTH * HEAD_DIM) ** (-0.5)
    grad_conv_x = sum((item[3] for item in outputs)) * norm_tokens
    grad_conv_bc = sum((item[4] for item in outputs)) * norm_tokens
    grad_skip = sum((item[5] for item in outputs)) * norm_skip
    return (y_output, grad_x, grad_bc, grad_conv_x, grad_conv_bc, grad_skip)
```

```python
import functools

import jax
import jax.numpy as jnp
from jax import lax
from jax.experimental import pallas as pl
from jax.experimental.pallas import tpu as pltpu
from jax.sharding import PartitionSpec as P

MESH = pl.DeviceIdType.MESH
f32 = jnp.float32
bf16 = jnp.bfloat16


def dot(a, b, ca, cb):
    return lax.dot_general(a, b, (((ca,), (cb,)), ((), ())), preferred_element_type=f32)


def expander(width, columns, head_dim):
    rows = lax.broadcasted_iota(jnp.int32, (2 * width, columns), 0) % width
    cols = lax.broadcasted_iota(jnp.int32, (2 * width, columns), 1) // head_dim
    return (rows == cols).astype(f32).astype(bf16)


def conv_taps(pad_ref, weight, first, tokens):
    total = weight[0:1, :] * pad_ref[pl.ds(first, tokens), :]
    for k in range(1, weight.shape[0]):
        total = total + weight[k : k + 1, :] * pad_ref[pl.ds(first + k, tokens), :]
    return total


def silu_parts(pre):
    sigma = jax.nn.sigmoid(pre)
    return pre * sigma, sigma * (1.0 + pre * (1.0 - sigma))


def state_kernel(
    head_dim, x_ref, halo_ref, bc_ref, bc_halo_ref, cw_ref, cbc_ref, fac_ref, g_ref,
    w_ref, inner_ref, ds_ref, s_ref, u_ref, mapped_ref, dsbc_ref, xp, bp,
):
    tokens, columns = x_ref.shape
    width = columns // head_dim
    n = mapped_ref.shape[1] // 2

    @pl.when(pl.program_id(0) == 0)
    def _():
        bp[0:8, :] = bc_halo_ref[...].astype(f32)
        bp[8 : 8 + tokens, :] = bc_ref[...].astype(f32)
        value, slope = silu_parts(conv_taps(bp, cbc_ref[...], 9 - cbc_ref.shape[0], tokens))
        mapped_ref[...] = value.astype(bf16)
        dsbc_ref[...] = slope

    xp[0:8, :] = halo_ref[...].astype(f32)
    xp[8 : 8 + tokens, :] = x_ref[...].astype(f32)
    value, slope = silu_parts(conv_taps(xp, cw_ref[...], 9 - cw_ref.shape[0], tokens))
    inner = value.astype(bf16)
    inner_ref[...] = inner
    ds_ref[...] = slope.astype(bf16)
    spread = dot(fac_ref[0], expander(width, columns, head_dim), 1, 0)
    w = (inner.astype(f32) * spread[:tokens]).astype(bf16)
    w_ref[...] = w
    lead = (g_ref[...].astype(f32) * spread[tokens : 2 * tokens]).astype(bf16)
    tail = (w.astype(f32) * spread[2 * tokens :]).astype(bf16)
    s_ref[0] = dot(mapped_ref[:, :n], tail, 0, 0).astype(bf16)
    u_ref[0] = dot(mapped_ref[:, n:], lead, 0, 0).astype(bf16)


def carry_kernel(
    devices, s_ref, u_ref, et_ref, p_ref, q_ref, out_f, out_b, send_f, recv_f, send_b, recv_b
):
    me = lax.axis_index("seq")
    chunks = s_ref.shape[0]
    barrier = pltpu.get_barrier_semaphore()
    for other in (lax.rem(me + 1, devices), lax.rem(me + devices - 1, devices)):
        pl.semaphore_signal(barrier, inc=1, device_id={"seq": other}, device_id_type=MESH)
    pl.semaphore_wait(barrier, 2)

    def forward(c):
        return pltpu.make_async_remote_copy(
            src_ref=out_f.at[c], dst_ref=p_ref.at[c], send_sem=send_f.at[c],
            recv_sem=recv_f.at[c], device_id={"seq": me + 1}, device_id_type=MESH,
        )

    def backward(c):
        return pltpu.make_async_remote_copy(
            src_ref=out_b.at[c], dst_ref=q_ref.at[c], send_sem=send_b.at[c],
            recv_sem=recv_b.at[c], device_id={"seq": me - 1}, device_id_type=MESH,
        )

    def advance(c, place, make, own_ref, in_ref, out_ref):
        @pl.when(place == 0)
        def _():
            in_ref[c] = jnp.zeros(in_ref.shape[1:], in_ref.dtype)
            out_ref[c] = own_ref[c]

        @pl.when(place > 0)
        def _():
            make(c).wait_recv()
            out_ref[c] = (in_ref[c].astype(f32) * et_ref[c] + own_ref[c].astype(f32)).astype(bf16)

        @pl.when(place < devices - 1)
        def _():
            make(c).start()

    back = devices - 1 - me

    @pl.loop(0, chunks + devices - 1)
    def _(step):
        cf = step - me
        cb = step - back

        @pl.when((cf >= 0) & (cf < chunks))
        def _():
            advance(cf, me, forward, s_ref, p_ref, out_f)

        @pl.when((cb >= 0) & (cb < chunks))
        def _():
            advance(cb, back, backward, u_ref, q_ref, out_b)

    @pl.loop(0, chunks)
    def _(c):
        @pl.when(me < devices - 1)
        def _():
            forward(c).wait_send()

        @pl.when(me > 0)
        def _():
            backward(c).wait_send()


def apply_kernel(
    head_dim, scale, x_ref, halo_ref, cw_ref, fac_ref, ct_ref, cr_ref, skip_ref, g_ref, w_ref,
    inner_ref, ds_ref, mapped_ref, dsbc_ref, p_ref, q_ref,
    y_ref, gx_ref, edge_ref, taps_ref, dbc_ref, sim, dsim, dbc, xp, dp, ya, da,
):
    tokens, columns = x_ref.shape
    width = columns // head_dim
    n = mapped_ref.shape[1] // 2
    taps = cw_ref.shape[0]
    lower = lax.broadcasted_iota(jnp.int32, (tokens, tokens), 0) >= lax.broadcasted_iota(
        jnp.int32, (tokens, tokens), 1
    )
    b_mat = mapped_ref[:, :n]
    c_mat = mapped_ref[:, n:]

    @pl.when(pl.program_id(0) == 0)
    def _():
        sim[...] = dot(c_mat, b_mat, 1, 1)
        dsim[...] = jnp.zeros_like(dsim)
        dbc[...] = jnp.zeros_like(dbc)

    pair = 2 * head_dim
    side = lax.broadcasted_iota(jnp.int32, (1, pair), 1) < head_dim
    for j in range(width // 2):
        cols = slice(j * pair, (j + 1) * pair)
        w_pair = w_ref[:, cols]
        g_pair = g_ref[:, cols]
        parts = []
        for e in range(2):
            h = 2 * j + e
            diff = ct_ref[0, :, h : h + 1] - cr_ref[0, h : h + 1, :]
            decay = jnp.exp(jnp.where(lower, diff, -1e30))
            mix = (decay * sim[...]).astype(bf16)
            mine = side if e == 0 else jnp.logical_not(side)
            g_own = jnp.where(mine, g_pair.astype(f32), 0.0).astype(bf16)
            dsim[...] += decay * dot(g_own, w_pair, 1, 1)
            parts.append((dot(mix, w_pair, 1, 0), dot(mix, g_pair, 0, 0)))
        ya[:, cols] = jnp.where(side, parts[0][0], parts[1][0])
        da[:, cols] = jnp.where(side, parts[0][1], parts[1][1])

    spread = dot(fac_ref[0], expander(width, columns, head_dim), 1, 0)
    gain = spread[:tokens]
    lead = spread[tokens : 2 * tokens]
    tail = spread[2 * tokens :]
    g = g_ref[...].astype(f32)
    inner = inner_ref[...].astype(f32)
    p = p_ref[0]
    q = q_ref[0]
    y = scale * (ya[...] + lead * dot(c_mat, p, 1, 0)) + skip_ref[...] * inner
    y_ref[...] = y.astype(bf16)
    d_w = scale * (da[...] + tail * dot(b_mat, q, 1, 0))
    d_pre = (gain * d_w + skip_ref[...] * g) * ds_ref[...].astype(f32)
    dbc[:, :n] += dot((w_ref[...].astype(f32) * tail).astype(bf16), q, 1, 1)
    dbc[:, n:] += dot((g * lead).astype(bf16), p, 1, 1)

    xp[0:8, :] = halo_ref[...].astype(f32)
    xp[8 : 8 + tokens, :] = x_ref[...].astype(f32)
    dp[0:tokens, :] = d_pre
    dp[tokens : tokens + 8, :] = jnp.zeros((8, columns), f32)
    total = jnp.zeros((tokens, columns), f32)
    for k in range(taps):
        total = total + cw_ref[k : k + 1, :] * dp[pl.ds(taps - 1 - k, tokens), :]
        taps_ref[k : k + 1, :] = jnp.sum(
            d_pre * xp[pl.ds(9 - taps + k, tokens), :], axis=0, keepdims=True
        )
    gx_ref[...] = total.astype(bf16)
    taps_ref[taps : taps + 1, :] = jnp.sum(g * inner, axis=0, keepdims=True)
    taps_ref[taps + 1 :, :] = jnp.zeros((8 - taps - 1, columns), f32)
    edge_ref[...] = d_pre[0:8]

    @pl.when(pl.program_id(0) == pl.num_programs(0) - 1)
    def _():
        d_sim = dsim[...].astype(bf16)
        d_b = dbc[:, :n] + dot(d_sim, c_mat, 0, 0)
        d_c = dbc[:, n:] + dot(d_sim, b_mat, 1, 0)
        dbc_ref[:, :n] = scale * d_b * dsbc_ref[:, :n]
        dbc_ref[:, n:] = scale * d_c * dsbc_ref[:, n:]


def shifted(block, axis, distance):
    devices = range(lax.axis_size(axis))
    route = [(i - distance, i) for i in devices if i - distance in devices]
    return lax.ppermute(block, axis, route)


def local(x_input, bc_input, decays, conv_x, conv_bc, skip_gain, grad_out):
    x = x_input[0]
    bc = bc_input[0]
    d = decays[0]
    g = grad_out[0]
    tokens, channels = x.shape
    taps = conv_x.shape[0]
    heads = d.shape[0]
    head_dim = channels // heads
    n = bc.shape[1] // 2
    scale = float(n) ** (-0.5)
    seq = lax.axis_size("seq")
    width = next(k for k in (8, 4, 2) if heads % k == 0)
    groups = heads // width
    columns = width * head_dim

    halo = shifted(jnp.concatenate([x[tokens - 8 :], bc[tokens - 8 :]], axis=1), "seq", 1)
    halo_x = halo[:, :channels]
    halo_bc = halo[:, channels:]

    cum = jnp.cumsum(jnp.log(d), axis=1)
    total = cum[:, -1:]
    factors = jnp.stack([jnp.sqrt((1.0 - d) * (1.0 + d)), jnp.exp(cum), jnp.exp(total - cum)])
    factors = factors.reshape(3, groups, width, tokens).transpose(1, 0, 3, 2)
    factors = factors.reshape(groups, 3 * tokens, width)
    high = lax.reduce_precision(factors, 8, 7)
    fac = jnp.concatenate([high.astype(bf16), (factors - high).astype(bf16)], axis=2)
    cum_r = cum.reshape(groups, width, tokens)
    cum_t = cum_r.transpose(0, 2, 1)
    et = jnp.repeat(jnp.exp(total[:, 0]), head_dim).reshape(groups, 1, columns)
    skip = jnp.repeat(skip_gain, head_dim)[None, :]

    def cols(rows):
        return pl.BlockSpec((rows, columns), lambda i: (0, i))

    def whole(rows, c):
        return pl.BlockSpec((rows, c), lambda i: (0, 0))

    def chunk(a, b):
        return pl.BlockSpec((1, a, b), lambda i: (i, 0, 0))

    def out(shape, dtype):
        return jax.ShapeDtypeStruct(shape, dtype)

    params = pltpu.CompilerParams(
        dimension_semantics=("arbitrary",), vmem_limit_bytes=48 * 1024 * 1024
    )
    w, inner, slope, s_own, u_own, mapped, slope_bc = pl.pallas_call(
        functools.partial(state_kernel, head_dim),
        grid=(groups,),
        in_specs=[
            cols(tokens), cols(8), whole(tokens, 2 * n), whole(8, 2 * n), cols(taps),
            whole(taps, 2 * n), chunk(3 * tokens, 2 * width), cols(tokens),
        ],
        out_specs=[
            cols(tokens), cols(tokens), cols(tokens), chunk(n, columns), chunk(n, columns),
            whole(tokens, 2 * n), whole(tokens, 2 * n),
        ],
        out_shape=[
            out((tokens, channels), bf16), out((tokens, channels), bf16),
            out((tokens, channels), bf16), out((groups, n, columns), bf16),
            out((groups, n, columns), bf16), out((tokens, 2 * n), bf16), out((tokens, 2 * n), f32),
        ],
        scratch_shapes=[
            pltpu.VMEM((tokens + 8, columns), f32), pltpu.VMEM((tokens + 8, 2 * n), f32),
        ],
        compiler_params=params,
        name="states",
    )(x, halo_x, bc, halo_bc, conv_x, conv_bc, fac, g)

    vmem = pl.BlockSpec(memory_space=pltpu.VMEM)
    p_in, q_in = pl.pallas_call(
        functools.partial(carry_kernel, seq),
        in_specs=[vmem] * 3,
        out_specs=[vmem] * 2,
        out_shape=[out((groups, n, columns), bf16)] * 2,
        scratch_shapes=[pltpu.VMEM((groups, n, columns), bf16)] * 2
        + [pltpu.SemaphoreType.DMA((groups,))] * 4,
        compiler_params=pltpu.CompilerParams(
            collective_id=0, has_side_effects=True, vmem_limit_bytes=32 * 1024 * 1024
        ),
        name="carry",
    )(s_own, u_own, et)

    y, gx, edge, taps_part, d_bc = pl.pallas_call(
        functools.partial(apply_kernel, head_dim, scale),
        grid=(groups,),
        in_specs=[
            cols(tokens), cols(8), cols(taps), chunk(3 * tokens, 2 * width),
            chunk(tokens, width), chunk(width, tokens), cols(1), cols(tokens), cols(tokens),
            cols(tokens), cols(tokens), whole(tokens, 2 * n), whole(tokens, 2 * n),
            chunk(n, columns), chunk(n, columns),
        ],
        out_specs=[cols(tokens), cols(tokens), cols(8), cols(8), whole(tokens, 2 * n)],
        out_shape=[
            out((tokens, channels), bf16), out((tokens, channels), bf16), out((8, channels), f32),
            out((8, channels), f32), out((tokens, 2 * n), f32),
        ],
        scratch_shapes=[
            pltpu.VMEM((tokens, tokens), f32), pltpu.VMEM((tokens, tokens), f32),
            pltpu.VMEM((tokens, 2 * n), f32), pltpu.VMEM((tokens + 8, columns), f32),
            pltpu.VMEM((tokens + 8, columns), f32), pltpu.VMEM((tokens, columns), f32),
            pltpu.VMEM((tokens, columns), f32),
        ],
        compiler_params=params,
        name="apply",
    )(
        x, halo_x, conv_x, fac, cum_t, cum_r, skip, g, w, inner, slope, mapped, slope_bc, p_in, q_in
    )

    d_bc = lax.psum(d_bc, "head")
    next_rows = shifted(jnp.concatenate([edge, d_bc[:8]], axis=1), "seq", -1)

    def fix(rows_out, next_part, weight):
        last = []
        for r in range(taps - 1):
            row = jnp.zeros((1, weight.shape[1]), f32)
            for k in range(r + 1):
                row = row + weight[k : k + 1] * next_part[r - k : r - k + 1]
            last.append(row)
        return jnp.concatenate(last, axis=0)

    fix_x = fix(gx, next_rows[:, :channels], conv_x)
    gx = gx.at[tokens - taps + 1 :].add(fix_x.astype(bf16))
    dpad = jnp.concatenate([d_bc, next_rows[: taps - 1, channels:]], axis=0)
    bpad = jnp.concatenate([halo_bc[8 - taps + 1 :], bc], axis=0).astype(f32)
    gbc = sum(conv_bc[k][None] * dpad[taps - 1 - k : taps - 1 - k + tokens] for k in range(taps))
    taps_bc = jnp.stack([jnp.sum(d_bc * bpad[k : k + tokens], axis=0) for k in range(taps)])
    taps_bc = jnp.pad(taps_bc, ((0, 8 - taps), (0, 0)))
    sums = lax.psum(jnp.concatenate([taps_part, taps_bc], axis=1), ("seq", "dp"))
    token_count = tokens * seq * lax.axis_size("dp")
    norm_tokens = float(token_count) ** (-0.5)
    norm_skip = float(token_count * head_dim) ** (-0.5)
    skip_sum = jnp.sum(sums[taps, :channels].reshape(heads, head_dim), axis=1)
    return (
        y[None],
        gx[None],
        gbc.astype(bf16)[None],
        sums[:taps, :channels] * norm_tokens,
        sums[:taps, channels:] * norm_tokens,
        skip_sum * norm_skip,
    )


def solution(mesh):
    return jax.shard_map(
        local,
        mesh=mesh,
        in_specs=(
            P(("groups", "dp"), "seq", "head"),
            P(("groups", "dp"), "seq", None),
            P(("groups", "dp"), "head", "seq"),
            P(None, "head"),
            P(),
            P("head"),
            P(("groups", "dp"), "seq", "head"),
        ),
        out_specs=(
            P(("groups", "dp"), "seq", "head"),
            P(("groups", "dp"), "seq", "head"),
            P(("groups", "dp"), "seq", None),
            P("groups", "head"),
            P("groups", None),
            P(("groups", "head")),
        ),
        check_vma=False,
    )
```

```python
import functools

import jax
import jax.numpy as jnp
from jax import lax
from jax.experimental import pallas as pl
from jax.experimental.pallas import tpu as pltpu
from jax.sharding import PartitionSpec as P

MESH = pl.DeviceIdType.MESH
f32 = jnp.float32
bf16 = jnp.bfloat16


def dot(a, b, ca, cb):
    return lax.dot_general(a, b, (((ca,), (cb,)), ((), ())), preferred_element_type=f32)


def expander(width, columns, head_dim):
    rows = lax.broadcasted_iota(jnp.int32, (2 * width, columns), 0) % width
    cols = lax.broadcasted_iota(jnp.int32, (2 * width, columns), 1) // head_dim
    return (rows == cols).astype(f32).astype(bf16)


def conv_taps(pad_ref, weight, first, tokens):
    total = weight[0:1, :] * pad_ref[pl.ds(first, tokens), :]
    for k in range(1, weight.shape[0]):
        total = total + weight[k : k + 1, :] * pad_ref[pl.ds(first + k, tokens), :]
    return total


def silu_parts(pre):
    sigma = jax.nn.sigmoid(pre)
    return pre * sigma, sigma * (1.0 + pre * (1.0 - sigma))


def state_kernel(
    head_dim, x_ref, halo_ref, bc_ref, bc_halo_ref, cw_ref, cbc_ref, fac_ref, g_ref,
    w_ref, inner_ref, ds_ref, s_ref, u_ref, mapped_ref, dsbc_ref, xp, bp,
):
    tokens, columns = x_ref.shape
    width = columns // head_dim
    n = mapped_ref.shape[1] // 2

    @pl.when(pl.program_id(0) == 0)
    def _():
        bp[0:8, :] = bc_halo_ref[...].astype(f32)
        bp[8 : 8 + tokens, :] = bc_ref[...].astype(f32)
        value, slope = silu_parts(conv_taps(bp, cbc_ref[...], 9 - cbc_ref.shape[0], tokens))
        mapped_ref[...] = value.astype(bf16)
        dsbc_ref[...] = slope

    xp[0:8, :] = halo_ref[...].astype(f32)
    xp[8 : 8 + tokens, :] = x_ref[...].astype(f32)
    value, slope = silu_parts(conv_taps(xp, cw_ref[...], 9 - cw_ref.shape[0], tokens))
    inner = value.astype(bf16)
    inner_ref[...] = inner
    ds_ref[...] = slope.astype(bf16)
    spread = dot(fac_ref[0], expander(width, columns, head_dim), 1, 0)
    w = (inner.astype(f32) * spread[:tokens]).astype(bf16)
    w_ref[...] = w
    lead = (g_ref[...].astype(f32) * spread[tokens : 2 * tokens]).astype(bf16)
    tail = (w.astype(f32) * spread[2 * tokens :]).astype(bf16)
    s_ref[0] = dot(mapped_ref[:, :n], tail, 0, 0).astype(bf16)
    u_ref[0] = dot(mapped_ref[:, n:], lead, 0, 0).astype(bf16)


def carry_kernel(
    devices, s_ref, u_ref, et_ref, p_ref, q_ref, out_f, out_b, send_f, recv_f, send_b, recv_b
):
    me = lax.axis_index("seq")
    chunks = s_ref.shape[0]
    barrier = pltpu.get_barrier_semaphore()
    for other in (lax.rem(me + 1, devices), lax.rem(me + devices - 1, devices)):
        pl.semaphore_signal(barrier, inc=1, device_id={"seq": other}, device_id_type=MESH)
    pl.semaphore_wait(barrier, 2)

    def forward(c):
        return pltpu.make_async_remote_copy(
            src_ref=out_f.at[c], dst_ref=p_ref.at[c], send_sem=send_f.at[c],
            recv_sem=recv_f.at[c], device_id={"seq": me + 1}, device_id_type=MESH,
        )

    def backward(c):
        return pltpu.make_async_remote_copy(
            src_ref=out_b.at[c], dst_ref=q_ref.at[c], send_sem=send_b.at[c],
            recv_sem=recv_b.at[c], device_id={"seq": me - 1}, device_id_type=MESH,
        )

    def advance(c, place, make, own_ref, in_ref, out_ref):
        @pl.when(place == 0)
        def _():
            in_ref[c] = jnp.zeros(in_ref.shape[1:], in_ref.dtype)
            out_ref[c] = own_ref[c]

        @pl.when(place > 0)
        def _():
            make(c).wait_recv()
            out_ref[c] = (in_ref[c].astype(f32) * et_ref[c] + own_ref[c].astype(f32)).astype(bf16)

        @pl.when(place < devices - 1)
        def _():
            make(c).start()

    back = devices - 1 - me

    @pl.loop(0, chunks + devices - 1)
    def _(step):
        cf = step - me
        cb = step - back

        @pl.when((cf >= 0) & (cf < chunks))
        def _():
            advance(cf, me, forward, s_ref, p_ref, out_f)

        @pl.when((cb >= 0) & (cb < chunks))
        def _():
            advance(cb, back, backward, u_ref, q_ref, out_b)

    @pl.loop(0, chunks)
    def _(c):
        @pl.when(me < devices - 1)
        def _():
            forward(c).wait_send()

        @pl.when(me > 0)
        def _():
            backward(c).wait_send()


def apply_kernel(
    head_dim, scale, x_ref, halo_ref, cw_ref, fac_ref, ct_ref, cr_ref, skip_ref, g_ref, w_ref,
    inner_ref, ds_ref, mapped_ref, dsbc_ref, p_ref, q_ref,
    y_ref, gx_ref, tail_ref, edge_ref, taps_ref, dbc_ref, sim, dsim, dbc, xp, dp, ya, da,
):
    tokens, columns = x_ref.shape
    width = columns // head_dim
    n = mapped_ref.shape[1] // 2
    taps = cw_ref.shape[0]
    lower = lax.broadcasted_iota(jnp.int32, (tokens, tokens), 0) >= lax.broadcasted_iota(
        jnp.int32, (tokens, tokens), 1
    )
    b_mat = mapped_ref[:, :n]
    c_mat = mapped_ref[:, n:]

    @pl.when(pl.program_id(0) == 0)
    def _():
        sim[...] = dot(c_mat, b_mat, 1, 1)
        dsim[...] = jnp.zeros_like(dsim)
        dbc[...] = jnp.zeros_like(dbc)

    pair = 2 * head_dim
    side = lax.broadcasted_iota(jnp.int32, (1, pair), 1) < head_dim
    for j in range(width // 2):
        cols = slice(j * pair, (j + 1) * pair)
        w_pair = w_ref[:, cols]
        g_pair = g_ref[:, cols]
        parts = []
        for e in range(2):
            h = 2 * j + e
            diff = ct_ref[0, :, h : h + 1] - cr_ref[0, h : h + 1, :]
            decay = jnp.exp(jnp.where(lower, diff, -1e30))
            mix = (decay * sim[...]).astype(bf16)
            mine = side if e == 0 else jnp.logical_not(side)
            g_own = jnp.where(mine, g_pair.astype(f32), 0.0).astype(bf16)
            dsim[...] += decay * dot(g_own, w_pair, 1, 1)
            parts.append((dot(mix, w_pair, 1, 0), dot(mix, g_pair, 0, 0)))
        ya[:, cols] = jnp.where(side, parts[0][0], parts[1][0])
        da[:, cols] = jnp.where(side, parts[0][1], parts[1][1])

    spread = dot(fac_ref[0], expander(width, columns, head_dim), 1, 0)
    gain = spread[:tokens]
    lead = spread[tokens : 2 * tokens]
    tail = spread[2 * tokens :]
    g = g_ref[...].astype(f32)
    inner = inner_ref[...].astype(f32)
    p = p_ref[0]
    q = q_ref[0]
    y = scale * (ya[...] + lead * dot(c_mat, p, 1, 0)) + skip_ref[...] * inner
    y_ref[...] = y.astype(bf16)
    d_w = scale * (da[...] + tail * dot(b_mat, q, 1, 0))
    d_pre = (gain * d_w + skip_ref[...] * g) * ds_ref[...].astype(f32)
    dbc[:, :n] += dot((w_ref[...].astype(f32) * tail).astype(bf16), q, 1, 1)
    dbc[:, n:] += dot((g * lead).astype(bf16), p, 1, 1)

    xp[0:8, :] = halo_ref[...].astype(f32)
    xp[8 : 8 + tokens, :] = x_ref[...].astype(f32)
    dp[0:tokens, :] = d_pre
    dp[tokens : tokens + 8, :] = jnp.zeros((8, columns), f32)
    total = jnp.zeros((tokens, columns), f32)
    for k in range(taps):
        total = total + cw_ref[k : k + 1, :] * dp[pl.ds(taps - 1 - k, tokens), :]
        taps_ref[k : k + 1, :] = jnp.sum(
            d_pre * xp[pl.ds(9 - taps + k, tokens), :], axis=0, keepdims=True
        )
    gx_ref[...] = total.astype(bf16)
    tail_ref[...] = total[tokens - 16 :]
    taps_ref[taps : taps + 1, :] = jnp.sum(g * inner, axis=0, keepdims=True)
    taps_ref[taps + 1 :, :] = jnp.zeros((8 - taps - 1, columns), f32)
    edge_ref[...] = d_pre[0:8]

    @pl.when(pl.program_id(0) == pl.num_programs(0) - 1)
    def _():
        d_sim = dsim[...].astype(bf16)
        d_b = dbc[:, :n] + dot(d_sim, c_mat, 0, 0)
        d_c = dbc[:, n:] + dot(d_sim, b_mat, 1, 0)
        dbc_ref[:, :n] = (scale * d_b * dsbc_ref[:, :n]).astype(bf16)
        dbc_ref[:, n:] = (scale * d_c * dsbc_ref[:, n:]).astype(bf16)


def finish_kernel(
    sizes, norm, tail_ref, edge_ref, taps_ref, dbc_ref, bc_ref, bc_halo_ref, cw_ref, cbc_ref,
    gbc_ref, gx_ref, sums_ref, bsum_ref, part, rs_in, red, ag_in, bct, bct_in, head_in, next_bc,
    next_x, bp, dp, rs_send, rs_recv, ag_send, ag_recv, bc_send, bc_recv, head_send, head_recv,
    edge_send, edge_recv, nbc_send, nbc_recv,
):
    seq, heads, cores = sizes
    members = seq * cores
    z = lax.axis_index("seq")
    hd = lax.axis_index("head")
    core = lax.axis_index("dp")
    me = z * cores + core
    tokens = dbc_ref.shape[0]
    taps = cw_ref.shape[0]
    channels = taps_ref.shape[1]
    share = part.shape[2]

    def member(offset):
        at = lax.rem(me + offset, members)
        return at, {"seq": at // cores, "dp": lax.rem(at, cores)}

    barrier = pltpu.get_barrier_semaphore()
    targets = [member(o)[1] for o in range(1, members)]
    for o in range(1, heads):
        other = lax.rem(hd + o, heads)
        targets.append({"head": other})
        targets.append({"head": other, "seq": lax.rem(z + 1, seq)})
        targets.append({"head": other, "seq": lax.rem(z + seq - 1, seq)})
    for target in targets:
        pl.semaphore_signal(barrier, inc=1, device_id=target, device_id_type=MESH)

    for i in range(members):
        low = min(i * share, channels)
        high = min(low + share, channels)
        if high - low < share:
            part[i] = jnp.zeros(part.shape[1:], f32)
        if high > low:
            part[i, :, 0 : high - low] = taps_ref[:, low:high]
    pl.semaphore_wait(barrier, len(targets))

    def head_copy(o):
        return pltpu.make_async_remote_copy(
            src_ref=dbc_ref, dst_ref=head_in.at[hd], send_sem=head_send.at[o],
            recv_sem=head_recv.at[hd], device_id={"head": lax.rem(hd + o, heads)},
            device_id_type=MESH,
        )

    def nbc_copy(o):
        return pltpu.make_async_remote_copy(
            src_ref=dbc_ref.at[0:16], dst_ref=next_bc.at[hd], send_sem=nbc_send.at[o],
            recv_sem=nbc_recv.at[hd],
            device_id={"head": lax.rem(hd + o, heads), "seq": z - 1}, device_id_type=MESH,
        )

    def edge_copy():
        return pltpu.make_async_remote_copy(
            src_ref=edge_ref, dst_ref=next_x, send_sem=edge_send, recv_sem=edge_recv,
            device_id={"seq": z - 1}, device_id_type=MESH,
        )

    def rs_copy(o):
        at, device = member(o)
        return pltpu.make_async_remote_copy(
            src_ref=part.at[at], dst_ref=rs_in.at[me], send_sem=rs_send.at[o],
            recv_sem=rs_recv.at[me], device_id=device, device_id_type=MESH,
        )

    def ag_copy(o):
        return pltpu.make_async_remote_copy(
            src_ref=red, dst_ref=ag_in.at[me], send_sem=ag_send.at[o],
            recv_sem=ag_recv.at[me], device_id=member(o)[1], device_id_type=MESH,
        )

    def bct_copy(o):
        return pltpu.make_async_remote_copy(
            src_ref=bct, dst_ref=bct_in.at[me], send_sem=bc_send.at[o],
            recv_sem=bc_recv.at[me], device_id=member(o)[1], device_id_type=MESH,
        )

    def arrived(slots, sem, at, source):
        pltpu.make_async_remote_copy(
            src_ref=source, dst_ref=slots.at[at], send_sem=sem.at[at], recv_sem=sem.at[at],
            device_id=member(1)[1], device_id_type=MESH,
        ).wait_recv()

    for o in range(1, heads):
        head_copy(o).start()
    for o in range(1, members):
        rs_copy(o).start()

    @pl.when(z > 0)
    def _():
        for o in range(heads):
            nbc_copy(o).start()
        edge_copy().start()

    head_in[hd] = dbc_ref[...]
    rs_in[me] = part[me]
    bp[0:8, :] = bc_halo_ref[...].astype(f32)
    bp[8 : 8 + tokens, :] = bc_ref[...].astype(f32)

    for o in range(1, heads):
        arrived(head_in, head_recv, lax.rem(hd + o, heads), dbc_ref)
    full = head_in[0].astype(f32)
    for h in range(1, heads):
        full = full + head_in[h].astype(f32)
    for k in range(taps):
        bct[k : k + 1, :] = jnp.sum(
            full * bp[pl.ds(9 - taps + k, tokens), :], axis=0, keepdims=True
        )
    bct[taps:, :] = jnp.zeros((8 - taps, bct.shape[1]), f32)
    for o in range(1, members):
        bct_copy(o).start()
    for o in range(1, members):
        arrived(rs_in, rs_recv, lax.rem(me + o, members), part.at[0])
    total = rs_in[0]
    for i in range(1, members):
        total = total + rs_in[i]
    red[...] = total
    for o in range(1, members):
        ag_copy(o).start()
    ag_in[me] = total
    bct_in[me] = bct[...]

    dp[0:tokens, :] = full
    gx_ref[...] = tail_ref[...].astype(bf16)

    @pl.when(z == seq - 1)
    def _():
        dp[tokens : tokens + 8, :] = jnp.zeros((8, full.shape[1]), f32)

    @pl.when(z < seq - 1)
    def _():
        for o in range(heads):
            arrived(next_bc, nbc_recv, o, dbc_ref.at[0:16])
        edge_copy().wait_recv()
        rows = next_bc[0].astype(f32)
        for h in range(1, heads):
            rows = rows + next_bc[h].astype(f32)
        dp[tokens : tokens + 8, :] = rows[0:8]
        at = lax.broadcasted_iota(jnp.int32, (16, 1), 0)
        fixed = tail_ref[...]
        for r in range(taps - 1):
            row = jnp.zeros((1, channels), f32)
            for k in range(r + 1):
                row = row + cw_ref[k : k + 1, :] * next_x[r - k : r - k + 1, :]
            fixed = fixed + jnp.where(at == 16 - (taps - 1) + r, row, 0.0)
        gx_ref[...] = fixed.astype(bf16)

    grad = jnp.zeros(full.shape, f32)
    for k in range(taps):
        grad = grad + cbc_ref[k : k + 1, :] * dp[pl.ds(taps - 1 - k, tokens), :]
    gbc_ref[...] = grad.astype(bf16)

    for o in range(1, members):
        at = lax.rem(me + o, members)
        arrived(ag_in, ag_recv, at, red)
        arrived(bct_in, bc_recv, at, bct)
    bsum = bct_in[0]
    for i in range(1, members):
        bsum = bsum + bct_in[i]
    bsum_ref[...] = bsum[0:taps] * norm
    for i in range(members):
        low = min(i * share, channels)
        high = min(low + share, channels)
        if high > low:
            sums_ref[:, low:high] = ag_in[i, :, 0 : high - low] * norm

    for o in range(1, heads):
        head_copy(o).wait_send()
    for o in range(1, members):
        rs_copy(o).wait_send()
        ag_copy(o).wait_send()
        bct_copy(o).wait_send()

    @pl.when(z > 0)
    def _():
        for o in range(heads):
            nbc_copy(o).wait_send()
        edge_copy().wait_send()


def shifted(block, axis, distance):
    devices = range(lax.axis_size(axis))
    route = [(i - distance, i) for i in devices if i - distance in devices]
    return lax.ppermute(block, axis, route)


def local(x_input, bc_input, decays, conv_x, conv_bc, skip_gain, grad_out):
    x = x_input[0]
    bc = bc_input[0]
    d = decays[0]
    g = grad_out[0]
    tokens, channels = x.shape
    taps = conv_x.shape[0]
    heads = d.shape[0]
    head_dim = channels // heads
    n = bc.shape[1] // 2
    scale = float(n) ** (-0.5)
    seq = lax.axis_size("seq")
    width = next(k for k in (8, 4, 2) if heads % k == 0)
    groups = heads // width
    columns = width * head_dim

    halo = shifted(jnp.concatenate([x[tokens - 8 :], bc[tokens - 8 :]], axis=1), "seq", 1)
    halo_x = halo[:, :channels]
    halo_bc = halo[:, channels:]

    cum = jnp.cumsum(jnp.log(d), axis=1)
    total = cum[:, -1:]
    factors = jnp.stack([jnp.sqrt((1.0 - d) * (1.0 + d)), jnp.exp(cum), jnp.exp(total - cum)])
    factors = factors.reshape(3, groups, width, tokens).transpose(1, 0, 3, 2)
    factors = factors.reshape(groups, 3 * tokens, width)
    high = lax.reduce_precision(factors, 8, 7)
    fac = jnp.concatenate([high.astype(bf16), (factors - high).astype(bf16)], axis=2)
    cum_r = cum.reshape(groups, width, tokens)
    cum_t = cum_r.transpose(0, 2, 1)
    et = jnp.repeat(jnp.exp(total[:, 0]), head_dim).reshape(groups, 1, columns)
    skip = jnp.repeat(skip_gain, head_dim)[None, :]

    def cols(rows):
        return pl.BlockSpec((rows, columns), lambda i: (0, i))

    def whole(rows, c):
        return pl.BlockSpec((rows, c), lambda i: (0, 0))

    def chunk(a, b):
        return pl.BlockSpec((1, a, b), lambda i: (i, 0, 0))

    def out(shape, dtype):
        return jax.ShapeDtypeStruct(shape, dtype)

    params = pltpu.CompilerParams(
        dimension_semantics=("arbitrary",), vmem_limit_bytes=48 * 1024 * 1024
    )
    w, inner, slope, s_own, u_own, mapped, slope_bc = pl.pallas_call(
        functools.partial(state_kernel, head_dim),
        grid=(groups,),
        in_specs=[
            cols(tokens), cols(8), whole(tokens, 2 * n), whole(8, 2 * n), cols(taps),
            whole(taps, 2 * n), chunk(3 * tokens, 2 * width), cols(tokens),
        ],
        out_specs=[
            cols(tokens), cols(tokens), cols(tokens), chunk(n, columns), chunk(n, columns),
            whole(tokens, 2 * n), whole(tokens, 2 * n),
        ],
        out_shape=[
            out((tokens, channels), bf16), out((tokens, channels), bf16),
            out((tokens, channels), bf16), out((groups, n, columns), bf16),
            out((groups, n, columns), bf16), out((tokens, 2 * n), bf16), out((tokens, 2 * n), f32),
        ],
        scratch_shapes=[
            pltpu.VMEM((tokens + 8, columns), f32), pltpu.VMEM((tokens + 8, 2 * n), f32),
        ],
        compiler_params=params,
        name="states",
    )(x, halo_x, bc, halo_bc, conv_x, conv_bc, fac, g)

    vmem = pl.BlockSpec(memory_space=pltpu.VMEM)
    p_in, q_in = pl.pallas_call(
        functools.partial(carry_kernel, seq),
        in_specs=[vmem] * 3,
        out_specs=[vmem] * 2,
        out_shape=[out((groups, n, columns), bf16)] * 2,
        scratch_shapes=[pltpu.VMEM((groups, n, columns), bf16)] * 2
        + [pltpu.SemaphoreType.DMA((groups,))] * 4,
        compiler_params=pltpu.CompilerParams(
            collective_id=0, has_side_effects=True, vmem_limit_bytes=32 * 1024 * 1024
        ),
        name="carry",
    )(s_own, u_own, et)

    y, gx, tail, edge, taps_part, d_bc = pl.pallas_call(
        functools.partial(apply_kernel, head_dim, scale),
        grid=(groups,),
        in_specs=[
            cols(tokens), cols(8), cols(taps), chunk(3 * tokens, 2 * width),
            chunk(tokens, width), chunk(width, tokens), cols(1), cols(tokens), cols(tokens),
            cols(tokens), cols(tokens), whole(tokens, 2 * n), whole(tokens, 2 * n),
            chunk(n, columns), chunk(n, columns),
        ],
        out_specs=[
            cols(tokens), cols(tokens), cols(16), cols(8), cols(8), whole(tokens, 2 * n)
        ],
        out_shape=[
            out((tokens, channels), bf16), out((tokens, channels), bf16), out((16, channels), f32),
            out((8, channels), f32), out((8, channels), f32), out((tokens, 2 * n), bf16),
        ],
        scratch_shapes=[
            pltpu.VMEM((tokens, tokens), f32), pltpu.VMEM((tokens, tokens), f32),
            pltpu.VMEM((tokens, 2 * n), f32), pltpu.VMEM((tokens + 8, columns), f32),
            pltpu.VMEM((tokens + 8, columns), f32), pltpu.VMEM((tokens, columns), f32),
            pltpu.VMEM((tokens, columns), f32),
        ],
        compiler_params=params,
        name="apply",
    )(
        x, halo_x, conv_x, fac, cum_t, cum_r, skip, g, w, inner, slope, mapped, slope_bc, p_in, q_in
    )

    head_devices = lax.axis_size("head")
    cores = lax.axis_size("dp")
    members = seq * cores
    share = 128 * -(-channels // (128 * members))
    norm = float(tokens * members) ** (-0.5)
    dma = pltpu.SemaphoreType.DMA
    gbc, gx_tail, sums, taps_bc = pl.pallas_call(
        functools.partial(finish_kernel, (seq, head_devices, cores), norm),
        in_specs=[vmem] * 8,
        out_specs=[vmem] * 4,
        out_shape=[
            out((tokens, 2 * n), bf16), out((16, channels), bf16), out((8, channels), f32),
            out((taps, 2 * n), f32),
        ],
        scratch_shapes=[
            pltpu.VMEM((members, 8, share), f32), pltpu.VMEM((members, 8, share), f32),
            pltpu.VMEM((8, share), f32), pltpu.VMEM((members, 8, share), f32),
            pltpu.VMEM((8, 2 * n), f32), pltpu.VMEM((members, 8, 2 * n), f32),
            pltpu.VMEM((head_devices, tokens, 2 * n), bf16),
            pltpu.VMEM((head_devices, 16, 2 * n), bf16), pltpu.VMEM((8, channels), f32),
            pltpu.VMEM((tokens + 8, 2 * n), f32), pltpu.VMEM((tokens + 8, 2 * n), f32),
        ]
        + [dma((members,))] * 6
        + [dma((head_devices,))] * 2
        + [dma] * 2
        + [dma((head_devices,))] * 2,
        compiler_params=pltpu.CompilerParams(
            collective_id=1, has_side_effects=True, vmem_limit_bytes=32 * 1024 * 1024
        ),
        name="finish",
    )(tail, edge, taps_part, d_bc, bc, halo_bc, conv_x, conv_bc)
    gx = lax.dynamic_update_slice(gx, gx_tail, (tokens - 16, 0))
    skip_sum = jnp.sum(sums[taps].reshape(heads, head_dim), axis=1)
    return (
        y[None],
        gx[None],
        gbc[None],
        sums[:taps],
        taps_bc,
        skip_sum * float(head_dim) ** (-0.5),
    )


def solution(mesh):
    return jax.shard_map(
        local,
        mesh=mesh,
        in_specs=(
            P(("groups", "dp"), "seq", "head"),
            P(("groups", "dp"), "seq", None),
            P(("groups", "dp"), "head", "seq"),
            P(None, "head"),
            P(),
            P("head"),
            P(("groups", "dp"), "seq", "head"),
        ),
        out_specs=(
            P(("groups", "dp"), "seq", "head"),
            P(("groups", "dp"), "seq", "head"),
            P(("groups", "dp"), "seq", None),
            P("groups", "head"),
            P("groups", None),
            P(("groups", "head")),
        ),
        check_vma=False,
    )
```

```python
import functools

import jax
import jax.numpy as jnp
from jax import lax
from jax.experimental import pallas as pl
from jax.experimental.pallas import tpu as pltpu
from jax.sharding import PartitionSpec as P

MESH = pl.DeviceIdType.MESH
f32 = jnp.float32
bf16 = jnp.bfloat16


def dot(a, b, ca, cb):
    return lax.dot_general(a, b, (((ca,), (cb,)), ((), ())), preferred_element_type=f32)


def expander(width, columns, head_dim):
    rows = lax.broadcasted_iota(jnp.int32, (2 * width, columns), 0) % width
    cols = lax.broadcasted_iota(jnp.int32, (2 * width, columns), 1) // head_dim
    return (rows == cols).astype(f32).astype(bf16)


def conv_taps(pad_ref, weight, first, tokens):
    total = weight[0:1, :] * pad_ref[pl.ds(first, tokens), :]
    for k in range(1, weight.shape[0]):
        total = total + weight[k : k + 1, :] * pad_ref[pl.ds(first + k, tokens), :]
    return total


def silu_parts(pre):
    sigma = jax.nn.sigmoid(pre)
    return pre * sigma, sigma * (1.0 + pre * (1.0 - sigma))


def main_kernel(
    head_dim, scale, seq, lag, x_ref, x_end_ref, bc_ref, bc_end_ref, d_ref, cw_ref, cbc_ref,
    skip_ref, g_ref, y_ref, gx_ref, tail_ref, edge_ref, taps_ref, dbc_ref, bc_halo_ref,
    w_all, in_all, ds_all, ya, da, s_all, u_all, p_all, q_all, et, fac, cum_r, cum_t, halo, halo_b,
    mapped, dsbc, bp, xp, dp, sim, dsim, dbc,
    halo_send, halo_recv, send_f, recv_f, send_b, recv_b,
):
    step = pl.program_id(0)
    groups = w_all.shape[0]
    tokens, columns = x_ref.shape
    width = columns // head_dim
    n = mapped.shape[1] // 2
    taps = cw_ref.shape[0]
    first = 17 - taps
    me = lax.axis_index("seq")
    back = seq - 1 - me

    def remote(src, dst, send, recv, distance):
        return pltpu.make_async_remote_copy(
            src_ref=src, dst_ref=dst, send_sem=send, recv_sem=recv,
            device_id={"seq": me + distance}, device_id_type=MESH,
        )

    def halo_x():
        return remote(x_end_ref, halo, halo_send.at[0], halo_recv.at[0], 1)

    def halo_bc():
        return remote(bc_end_ref, halo_b, halo_send.at[1], halo_recv.at[1], 1)

    def forward(c):
        return remote(s_all.at[c], p_all.at[c], send_f.at[c], recv_f.at[c], 1)

    def backward(c):
        return remote(u_all.at[c], q_all.at[c], send_b.at[c], recv_b.at[c], -1)

    def advance(c, place, make, own, incoming):
        @pl.when(place == 0)
        def _():
            incoming[c] = jnp.zeros(incoming.shape[1:], bf16)

        @pl.when(place > 0)
        def _():
            make(c).wait_recv()

            @pl.when(place < seq - 1)
            def _():
                own[c] = (incoming[c].astype(f32) * et[c] + own[c].astype(f32)).astype(bf16)

        @pl.when(place < seq - 1)
        def _():
            make(c).start()

    def chain(at):
        cf = at - lag * me
        cb = at - lag * back

        @pl.when((cf >= 0) & (cf < groups))
        def _():
            advance(cf, me, forward, s_all, p_all)

        @pl.when((cb >= 0) & (cb < groups))
        def _():
            advance(cb, back, backward, u_all, q_all)

    @pl.when(step == 0)
    def _():
        barrier = pltpu.get_barrier_semaphore()
        for other in (lax.rem(me + 1, seq), lax.rem(me + seq - 1, seq)):
            pl.semaphore_signal(barrier, inc=1, device_id={"seq": other}, device_id_type=MESH)
        pl.semaphore_wait(barrier, 2)

        @pl.when(me < seq - 1)
        def _():
            halo_bc().start()
            halo_x().start()

        @pl.when(me == 0)
        def _():
            halo_b[...] = jnp.zeros(halo_b.shape, bf16)
            halo[...] = jnp.zeros(halo.shape, bf16)

    @pl.when(step < groups)
    def _():
        c = step
        d = d_ref[0]
        la = jnp.log(d)
        upto = (
            lax.broadcasted_iota(jnp.int32, (tokens, tokens), 0)
            <= lax.broadcasted_iota(jnp.int32, (tokens, tokens), 1)
        ).astype(f32).astype(bf16)
        rest = la
        rows = jnp.zeros(la.shape, f32)
        turned = jnp.zeros((tokens, width), f32)
        for _ in range(3):
            piece = rest.astype(bf16)
            rest = rest - piece.astype(f32)
            rows = rows + dot(piece, upto, 1, 0)
            turned = turned + dot(upto, piece, 0, 1)
        cum_r[c] = rows
        cum_t[c] = turned
        last = rows[:, tokens - 1 :]
        factors = jnp.concatenate(
            [jnp.sqrt((1.0 - d) * (1.0 + d)), jnp.exp(rows), jnp.exp(last - rows)], axis=1
        )
        high = factors.astype(bf16).astype(f32)
        both = jnp.concatenate([high, factors - high], axis=0).astype(bf16)
        fac[c] = both
        spread = dot(both, expander(width, columns, head_dim), 0, 0)
        et[c] = spread[2 * tokens - 1 : 2 * tokens]

        @pl.when(step == 0)
        def _():
            @pl.when(me > 0)
            def _():
                halo_bc().wait_recv()

            bc_halo_ref[...] = halo_b[...]
            bp[0:16, :] = halo_b[...].astype(f32)
            bp[16:, :] = bc_ref[...].astype(f32)
            value, slope = silu_parts(conv_taps(bp, cbc_ref[...], first, tokens))
            mapped[...] = value.astype(bf16)
            dsbc[...] = slope

            @pl.when(me > 0)
            def _():
                halo_x().wait_recv()

        lanes = pl.ds(pl.multiple_of(c * columns, columns), columns)
        xp[0:16, :] = halo[:, lanes].astype(f32)
        xp[16:, :] = x_ref[...].astype(f32)
        value, slope = silu_parts(conv_taps(xp, cw_ref[...], first, tokens))
        inner = value.astype(bf16)
        in_all[c] = inner
        ds_all[c] = slope.astype(bf16)
        w = (inner.astype(f32) * spread[:tokens]).astype(bf16)
        w_all[c] = w
        lead = (g_ref[...].astype(f32) * spread[tokens : 2 * tokens]).astype(bf16)
        tail = (w.astype(f32) * spread[2 * tokens :]).astype(bf16)
        s_all[c] = dot(mapped[:, :n], tail, 0, 0).astype(bf16)
        u_all[c] = dot(mapped[:, n:], lead, 0, 0).astype(bf16)

    @pl.when(step < 2 * groups)
    def _():
        chain(step)

    @pl.when((step >= groups) & (step < 2 * groups))
    def _():
        c = step - groups

        @pl.when(c == 0)
        def _():
            sim[...] = dot(mapped[:, n:], mapped[:, :n], 1, 1)
            dsim[...] = jnp.zeros_like(dsim)
            dbc[...] = jnp.zeros_like(dbc)

        lower = lax.broadcasted_iota(jnp.int32, (tokens, tokens), 0) >= lax.broadcasted_iota(
            jnp.int32, (tokens, tokens), 1
        )
        pair = 2 * head_dim
        side = lax.broadcasted_iota(jnp.int32, (1, pair), 1) < head_dim
        for j in range(width // 2):
            cols = slice(j * pair, (j + 1) * pair)
            w_pair = w_all[c, :, cols]
            g_pair = g_ref[:, cols]
            parts = []
            for e in range(2):
                h = 2 * j + e
                diff = cum_t[c, :, h : h + 1] - cum_r[c, h : h + 1, :]
                decay = jnp.exp(jnp.where(lower, diff, -1e30))
                mix = (decay * sim[...]).astype(bf16)
                mine = side if e == 0 else jnp.logical_not(side)
                g_own = jnp.where(mine, g_pair.astype(f32), 0.0).astype(bf16)
                dsim[...] += decay * dot(g_own, w_pair, 1, 1)
                parts.append((dot(mix, w_pair, 1, 0), dot(mix, g_pair, 0, 0)))
            ya[c, :, cols] = jnp.where(side, parts[0][0], parts[1][0])
            da[c, :, cols] = jnp.where(side, parts[0][1], parts[1][1])

    @pl.when(step == 2 * groups)
    def _():
        for at in range(2 * groups, groups + lag * (seq - 1)):
            chain(at)

    @pl.when(step >= 2 * groups)
    def _():
        c = step - 2 * groups
        b_mat = mapped[:, :n]
        c_mat = mapped[:, n:]
        spread = dot(fac[c], expander(width, columns, head_dim), 0, 0)
        gain = spread[:tokens]
        lead = spread[tokens : 2 * tokens]
        tail = spread[2 * tokens :]
        g = g_ref[...].astype(f32)
        inner = in_all[c].astype(f32)
        p = p_all[c]
        q = q_all[c]
        y = scale * (ya[c] + lead * dot(c_mat, p, 1, 0)) + skip_ref[...] * inner
        y_ref[...] = y.astype(bf16)
        d_w = scale * (da[c] + tail * dot(b_mat, q, 1, 0))
        d_pre = (gain * d_w + skip_ref[...] * g) * ds_all[c].astype(f32)
        dbc[:, :n] += dot((w_all[c].astype(f32) * tail).astype(bf16), q, 1, 1)
        dbc[:, n:] += dot((g * lead).astype(bf16), p, 1, 1)

        lanes = pl.ds(pl.multiple_of(c * columns, columns), columns)
        xp[0:16, :] = halo[:, lanes].astype(f32)
        xp[16:, :] = x_ref[...].astype(f32)
        dp[0:tokens, :] = d_pre
        dp[tokens:, :] = jnp.zeros((8, columns), f32)
        total = jnp.zeros((tokens, columns), f32)
        for k in range(taps):
            total = total + cw_ref[k : k + 1, :] * dp[pl.ds(taps - 1 - k, tokens), :]
            taps_ref[k : k + 1, :] = jnp.sum(
                d_pre * xp[pl.ds(first + k, tokens), :], axis=0, keepdims=True
            )
        gx_ref[...] = total.astype(bf16)
        tail_ref[...] = total[tokens - 16 :]
        taps_ref[taps : taps + 1, :] = jnp.sum(g * inner, axis=0, keepdims=True)
        taps_ref[taps + 1 :, :] = jnp.zeros((8 - taps - 1, columns), f32)
        edge_ref[...] = d_pre[0:8]

    @pl.when(step == 3 * groups - 1)
    def _():
        d_sim = dsim[...].astype(bf16)
        d_b = dbc[:, :n] + dot(d_sim, mapped[:, n:], 0, 0)
        d_c = dbc[:, n:] + dot(d_sim, mapped[:, :n], 1, 0)
        dbc_ref[:, :n] = (scale * d_b * dsbc[:, :n]).astype(bf16)
        dbc_ref[:, n:] = (scale * d_c * dsbc[:, n:]).astype(bf16)

        @pl.when(me < seq - 1)
        def _():
            halo_bc().wait_send()
            halo_x().wait_send()

        @pl.loop(0, groups)
        def _(c):
            @pl.when(me < seq - 1)
            def _():
                forward(c).wait_send()

            @pl.when(me > 0)
            def _():
                backward(c).wait_send()


def finish_kernel(
    sizes, norm, tail_ref, edge_ref, taps_ref, dbc_ref, bc_ref, bc_halo_ref, cw_ref, cbc_ref,
    gbc_ref, gx_ref, sums_ref, bsum_ref, part, rs_in, red, ag_in, bct, bct_in, head_in, next_bc,
    next_x, bp, dp, rs_send, rs_recv, ag_send, ag_recv, bc_send, bc_recv, head_send, head_recv,
    edge_send, edge_recv, nbc_send, nbc_recv,
):
    seq, heads, cores = sizes
    members = seq * cores
    z = lax.axis_index("seq")
    hd = lax.axis_index("head")
    core = lax.axis_index("dp")
    me = z * cores + core
    tokens = dbc_ref.shape[0]
    taps = cw_ref.shape[0]
    channels = taps_ref.shape[1]
    share = part.shape[2]

    def member(offset):
        at = lax.rem(me + offset, members)
        return at, {"seq": at // cores, "dp": lax.rem(at, cores)}

    barrier = pltpu.get_barrier_semaphore()
    targets = [member(o)[1] for o in range(1, members)]
    for o in range(1, heads):
        other = lax.rem(hd + o, heads)
        targets.append({"head": other})
        targets.append({"head": other, "seq": lax.rem(z + 1, seq)})
        targets.append({"head": other, "seq": lax.rem(z + seq - 1, seq)})
    for target in targets:
        pl.semaphore_signal(barrier, inc=1, device_id=target, device_id_type=MESH)

    for i in range(members):
        low = min(i * share, channels)
        high = min(low + share, channels)
        if high - low < share:
            part[i] = jnp.zeros(part.shape[1:], f32)
        if high > low:
            part[i, :, 0 : high - low] = taps_ref[:, low:high]
    pl.semaphore_wait(barrier, len(targets))

    def head_copy(o):
        return pltpu.make_async_remote_copy(
            src_ref=dbc_ref, dst_ref=head_in.at[hd], send_sem=head_send.at[o],
            recv_sem=head_recv.at[hd], device_id={"head": lax.rem(hd + o, heads)},
            device_id_type=MESH,
        )

    def nbc_copy(o):
        return pltpu.make_async_remote_copy(
            src_ref=dbc_ref.at[0:16], dst_ref=next_bc.at[hd], send_sem=nbc_send.at[o],
            recv_sem=nbc_recv.at[hd],
            device_id={"head": lax.rem(hd + o, heads), "seq": z - 1}, device_id_type=MESH,
        )

    def edge_copy():
        return pltpu.make_async_remote_copy(
            src_ref=edge_ref, dst_ref=next_x, send_sem=edge_send, recv_sem=edge_recv,
            device_id={"seq": z - 1}, device_id_type=MESH,
        )

    def rs_copy(o):
        at, device = member(o)
        return pltpu.make_async_remote_copy(
            src_ref=part.at[at], dst_ref=rs_in.at[me], send_sem=rs_send.at[o],
            recv_sem=rs_recv.at[me], device_id=device, device_id_type=MESH,
        )

    def ag_copy(o):
        return pltpu.make_async_remote_copy(
            src_ref=red, dst_ref=ag_in.at[me], send_sem=ag_send.at[o],
            recv_sem=ag_recv.at[me], device_id=member(o)[1], device_id_type=MESH,
        )

    def bct_copy(o):
        return pltpu.make_async_remote_copy(
            src_ref=bct, dst_ref=bct_in.at[me], send_sem=bc_send.at[o],
            recv_sem=bc_recv.at[me], device_id=member(o)[1], device_id_type=MESH,
        )

    def arrived(slots, sem, at, source):
        pltpu.make_async_remote_copy(
            src_ref=source, dst_ref=slots.at[at], send_sem=sem.at[at], recv_sem=sem.at[at],
            device_id=member(1)[1], device_id_type=MESH,
        ).wait_recv()

    for o in range(1, heads):
        head_copy(o).start()
    for o in range(1, members):
        rs_copy(o).start()

    @pl.when(z > 0)
    def _():
        for o in range(heads):
            nbc_copy(o).start()
        edge_copy().start()

    head_in[hd] = dbc_ref[...]
    rs_in[me] = part[me]
    bp[0:16, :] = bc_halo_ref[...].astype(f32)
    bp[16:, :] = bc_ref[...].astype(f32)

    for o in range(1, heads):
        arrived(head_in, head_recv, lax.rem(hd + o, heads), dbc_ref)
    full = head_in[0].astype(f32)
    for h in range(1, heads):
        full = full + head_in[h].astype(f32)
    for k in range(taps):
        bct[k : k + 1, :] = jnp.sum(
            full * bp[pl.ds(17 - taps + k, tokens), :], axis=0, keepdims=True
        )
    bct[taps:, :] = jnp.zeros((8 - taps, bct.shape[1]), f32)
    for o in range(1, members):
        bct_copy(o).start()
    for o in range(1, members):
        arrived(rs_in, rs_recv, lax.rem(me + o, members), part.at[0])
    total = rs_in[0]
    for i in range(1, members):
        total = total + rs_in[i]
    red[...] = total
    for o in range(1, members):
        ag_copy(o).start()
    ag_in[me] = total
    bct_in[me] = bct[...]

    dp[0:tokens, :] = full
    gx_ref[...] = tail_ref[...].astype(bf16)

    @pl.when(z == seq - 1)
    def _():
        dp[tokens : tokens + 8, :] = jnp.zeros((8, full.shape[1]), f32)

    @pl.when(z < seq - 1)
    def _():
        for o in range(heads):
            arrived(next_bc, nbc_recv, o, dbc_ref.at[0:16])
        edge_copy().wait_recv()
        rows = next_bc[0].astype(f32)
        for h in range(1, heads):
            rows = rows + next_bc[h].astype(f32)
        dp[tokens : tokens + 8, :] = rows[0:8]
        at = lax.broadcasted_iota(jnp.int32, (16, 1), 0)
        fixed = tail_ref[...]
        for r in range(taps - 1):
            row = jnp.zeros((1, channels), f32)
            for k in range(r + 1):
                row = row + cw_ref[k : k + 1, :] * next_x[r - k : r - k + 1, :]
            fixed = fixed + jnp.where(at == 16 - (taps - 1) + r, row, 0.0)
        gx_ref[...] = fixed.astype(bf16)

    grad = jnp.zeros(full.shape, f32)
    for k in range(taps):
        grad = grad + cbc_ref[k : k + 1, :] * dp[pl.ds(taps - 1 - k, tokens), :]
    gbc_ref[...] = grad.astype(bf16)

    for o in range(1, members):
        at = lax.rem(me + o, members)
        arrived(ag_in, ag_recv, at, red)
        arrived(bct_in, bc_recv, at, bct)
    bsum = bct_in[0]
    for i in range(1, members):
        bsum = bsum + bct_in[i]
    bsum_ref[...] = bsum[0:taps] * norm
    for i in range(members):
        low = min(i * share, channels)
        high = min(low + share, channels)
        if high > low:
            sums_ref[:, low:high] = ag_in[i, :, 0 : high - low] * norm

    for o in range(1, heads):
        head_copy(o).wait_send()
    for o in range(1, members):
        rs_copy(o).wait_send()
        ag_copy(o).wait_send()
        bct_copy(o).wait_send()

    @pl.when(z > 0)
    def _():
        for o in range(heads):
            nbc_copy(o).wait_send()
        edge_copy().wait_send()


def shifted(block, axis, distance):
    devices = range(lax.axis_size(axis))
    route = [(i - distance, i) for i in devices if i - distance in devices]
    return lax.ppermute(block, axis, route)


def local(x_input, bc_input, decays, conv_x, conv_bc, skip_gain, grad_out):
    x = x_input[0]
    bc = bc_input[0]
    d = decays[0]
    g = grad_out[0]
    tokens, channels = x.shape
    taps = conv_x.shape[0]
    heads = d.shape[0]
    head_dim = channels // heads
    n = bc.shape[1] // 2
    scale = float(n) ** (-0.5)
    seq = lax.axis_size("seq")
    width = next(k for k in (8, 4, 2) if heads % k == 0)
    groups = heads // width
    columns = width * head_dim

    decay_rows = d.reshape(groups, width, tokens)
    skip = jnp.repeat(skip_gain, head_dim)[None, :]

    def cols(rows):
        return pl.BlockSpec((rows, columns), lambda i: (0, lax.rem(i, groups)))

    def late(rows):
        return pl.BlockSpec((rows, columns), lambda i: (0, lax.max(i - 2 * groups, 0)))

    def whole(rows, c, at=0):
        return pl.BlockSpec((rows, c), lambda i: (at, 0))

    def out(shape, dtype):
        return jax.ShapeDtypeStruct(shape, dtype)

    dma = pltpu.SemaphoreType.DMA
    vmem = pl.BlockSpec(memory_space=pltpu.VMEM)
    wide = (groups, tokens, columns)
    y, gx, tail, edge, taps_part, d_bc, halo_bc = pl.pallas_call(
        functools.partial(main_kernel, head_dim, scale, seq, 2),
        grid=(3 * groups,),
        in_specs=[
            cols(tokens), whole(16, channels, tokens // 16 - 1), whole(tokens, 2 * n),
            whole(16, 2 * n, tokens // 16 - 1),
            pl.BlockSpec((1, width, tokens), lambda i: (lax.rem(i, groups), 0, 0)),
            cols(taps), whole(taps, 2 * n), cols(1), cols(tokens),
        ],
        out_specs=[
            late(tokens), late(tokens), late(16), late(8), late(8), whole(tokens, 2 * n),
            whole(16, 2 * n),
        ],
        out_shape=[
            out((tokens, channels), bf16), out((tokens, channels), bf16), out((16, channels), f32),
            out((8, channels), f32), out((8, channels), f32), out((tokens, 2 * n), bf16),
            out((16, 2 * n), bf16),
        ],
        scratch_shapes=[
            pltpu.VMEM(wide, bf16), pltpu.VMEM(wide, bf16), pltpu.VMEM(wide, bf16),
            pltpu.VMEM(wide, f32), pltpu.VMEM(wide, f32),
            pltpu.VMEM((groups, n, columns), bf16), pltpu.VMEM((groups, n, columns), bf16),
            pltpu.VMEM((groups, n, columns), bf16), pltpu.VMEM((groups, n, columns), bf16),
            pltpu.VMEM((groups, 1, columns), f32), pltpu.VMEM((groups, 2 * width, 3 * tokens), bf16),
            pltpu.VMEM((groups, width, tokens), f32), pltpu.VMEM((groups, tokens, width), f32),
            pltpu.VMEM((16, channels), bf16), pltpu.VMEM((16, 2 * n), bf16),
            pltpu.VMEM((tokens, 2 * n), bf16),
            pltpu.VMEM((tokens, 2 * n), f32), pltpu.VMEM((tokens + 16, 2 * n), f32),
            pltpu.VMEM((tokens + 16, columns), f32), pltpu.VMEM((tokens + 8, columns), f32),
            pltpu.VMEM((tokens, tokens), f32), pltpu.VMEM((tokens, tokens), f32),
            pltpu.VMEM((tokens, 2 * n), f32),
            dma((2,)), dma((2,)),
            dma((groups,)), dma((groups,)), dma((groups,)), dma((groups,)),
        ],
        compiler_params=pltpu.CompilerParams(
            dimension_semantics=("arbitrary",), vmem_limit_bytes=48 * 1024 * 1024,
            collective_id=0, has_side_effects=True,
        ),
        name="main",
    )(x, x, bc, bc, decay_rows, conv_x, conv_bc, skip, g)

    head_devices = lax.axis_size("head")
    cores = lax.axis_size("dp")
    members = seq * cores
    share = 128 * -(-channels // (128 * members))
    norm = float(tokens * members) ** (-0.5)
    gbc, gx_tail, sums, taps_bc = pl.pallas_call(
        functools.partial(finish_kernel, (seq, head_devices, cores), norm),
        in_specs=[vmem] * 8,
        out_specs=[vmem] * 4,
        out_shape=[
            out((tokens, 2 * n), bf16), out((16, channels), bf16), out((8, channels), f32),
            out((taps, 2 * n), f32),
        ],
        scratch_shapes=[
            pltpu.VMEM((members, 8, share), f32), pltpu.VMEM((members, 8, share), f32),
            pltpu.VMEM((8, share), f32), pltpu.VMEM((members, 8, share), f32),
            pltpu.VMEM((8, 2 * n), f32), pltpu.VMEM((members, 8, 2 * n), f32),
            pltpu.VMEM((head_devices, tokens, 2 * n), bf16),
            pltpu.VMEM((head_devices, 16, 2 * n), bf16), pltpu.VMEM((8, channels), f32),
            pltpu.VMEM((tokens + 16, 2 * n), f32), pltpu.VMEM((tokens + 8, 2 * n), f32),
        ]
        + [dma((members,))] * 6
        + [dma((head_devices,))] * 2
        + [dma] * 2
        + [dma((head_devices,))] * 2,
        compiler_params=pltpu.CompilerParams(
            collective_id=1, has_side_effects=True, vmem_limit_bytes=32 * 1024 * 1024
        ),
        name="finish",
    )(tail, edge, taps_part, d_bc, bc, halo_bc, conv_x, conv_bc)
    gx = lax.dynamic_update_slice(gx, gx_tail, (tokens - 16, 0))
    skip_sum = jnp.sum(sums[taps].reshape(heads, head_dim), axis=1)
    return (
        y[None],
        gx[None],
        gbc[None],
        sums[:taps],
        taps_bc,
        skip_sum * float(head_dim) ** (-0.5),
    )


def solution(mesh):
    return jax.shard_map(
        local,
        mesh=mesh,
        in_specs=(
            P(("groups", "dp"), "seq", "head"),
            P(("groups", "dp"), "seq", None),
            P(("groups", "dp"), "head", "seq"),
            P(None, "head"),
            P(),
            P("head"),
            P(("groups", "dp"), "seq", "head"),
        ),
        out_specs=(
            P(("groups", "dp"), "seq", "head"),
            P(("groups", "dp"), "seq", "head"),
            P(("groups", "dp"), "seq", None),
            P("groups", "head"),
            P("groups", None),
            P(("groups", "head")),
        ),
        check_vma=False,
    )
```

```python
import functools

import jax
import jax.numpy as jnp
from jax import lax
from jax.experimental import pallas as pl
from jax.experimental.pallas import tpu as pltpu
from jax.sharding import PartitionSpec as P

MESH = pl.DeviceIdType.MESH
f32 = jnp.float32
bf16 = jnp.bfloat16


def dot(a, b, ca, cb):
    return lax.dot_general(a, b, (((ca,), (cb,)), ((), ())), preferred_element_type=f32)


def expander(width, columns, head_dim):
    rows = lax.broadcasted_iota(jnp.int32, (2 * width, columns), 0) % width
    cols = lax.broadcasted_iota(jnp.int32, (2 * width, columns), 1) // head_dim
    return (rows == cols).astype(f32).astype(bf16)


def conv_taps(pad_ref, weight, first, tokens):
    total = weight[0:1, :] * pad_ref[pl.ds(first, tokens), :]
    for k in range(1, weight.shape[0]):
        total = total + weight[k : k + 1, :] * pad_ref[pl.ds(first + k, tokens), :]
    return total


def silu_parts(pre):
    sigma = jax.nn.sigmoid(pre)
    return pre * sigma, sigma * (1.0 + pre * (1.0 - sigma))


def main_kernel(
    head_dim, scale, norm, sizes, lag, x_ref, x_end_ref, bc_ref, bc_end_ref, d_ref, cw_ref,
    cw_all_ref, cbc_ref, skip_ref, g_ref, y_ref, gx_ref, gbc_ref, sums_ref, skips_ref, bsum_ref,
    w_all, in_all, ds_all, ya, da, s_all, u_all, p_all, q_all, et, fac, cum_r, cum_t, halo, halo_b,
    mapped, dsbc, bp, xp, dp, sim, dsim, dbc,
    tails, edges, parts_x, next_x, rs_in, ag_in, bct, bct_in, dbc_out, head_in, next_bc, dbp,
    halo_send, halo_recv, send_f, recv_f, send_b, recv_b,
    edge_send, edge_recv, rs_send, rs_recv, ag_send, ag_recv, bct_send, bct_recv,
    head_send, head_recv, nbc_send, nbc_recv,
):
    step = pl.program_id(0)
    groups = w_all.shape[0]
    tokens, columns = x_ref.shape
    width = columns // head_dim
    n = mapped.shape[1] // 2
    taps = cw_ref.shape[0]
    first = 17 - taps
    seq, heads, cores = sizes
    members = seq * cores
    me = lax.axis_index("seq")
    back = seq - 1 - me
    hd = lax.axis_index("head")
    place = me * cores + lax.axis_index("dp")

    def member(offset):
        at = lax.rem(place + offset, members)
        return at, {"seq": at // cores, "dp": lax.rem(at, cores)}

    def copy(src, dst, send, recv, device):
        return pltpu.make_async_remote_copy(
            src_ref=src, dst_ref=dst, send_sem=send, recv_sem=recv, device_id=device,
            device_id_type=MESH,
        )

    def head_copy(o):
        return copy(
            dbc_out, head_in.at[hd], head_send.at[o], head_recv.at[hd],
            {"head": lax.rem(hd + o, heads)},
        )

    def nbc_copy(o):
        return copy(
            dbc_out.at[0:16], next_bc.at[hd], nbc_send.at[o], nbc_recv.at[hd],
            {"head": lax.rem(hd + o, heads), "seq": me - 1},
        )

    def edge_copy(c):
        return copy(
            edges.at[c], next_x.at[c], edge_send.at[c], edge_recv.at[c], {"seq": me - 1}
        )

    def rs_copy(c):
        owner = lax.rem(c, members)
        return copy(
            parts_x.at[c], rs_in.at[c, place], rs_send.at[c], rs_recv.at[c, place],
            {"seq": owner // cores, "dp": lax.rem(owner, cores)},
        )

    def ag_copy(c, o):
        return copy(ag_in.at[c], ag_in.at[c], ag_send.at[c, o], ag_recv.at[c], member(o)[1])

    def bct_copy(o):
        return copy(bct, bct_in.at[place], bct_send.at[o], bct_recv.at[place], member(o)[1])

    def arrived(dst, sem, source):
        copy(source, dst, sem, sem, member(1)[1]).wait_recv()

    def remote(src, dst, send, recv, distance):
        return pltpu.make_async_remote_copy(
            src_ref=src, dst_ref=dst, send_sem=send, recv_sem=recv,
            device_id={"seq": me + distance}, device_id_type=MESH,
        )

    def halo_x():
        return remote(x_end_ref, halo, halo_send.at[0], halo_recv.at[0], 1)

    def halo_bc():
        return remote(bc_end_ref, halo_b, halo_send.at[1], halo_recv.at[1], 1)

    def forward(c):
        return remote(s_all.at[c], p_all.at[c], send_f.at[c], recv_f.at[c], 1)

    def backward(c):
        return remote(u_all.at[c], q_all.at[c], send_b.at[c], recv_b.at[c], -1)

    def advance(c, hops, make, own, incoming):
        @pl.when(hops == 0)
        def _():
            incoming[c] = jnp.zeros(incoming.shape[1:], bf16)

        @pl.when(hops > 0)
        def _():
            make(c).wait_recv()

            @pl.when(hops < seq - 1)
            def _():
                own[c] = (incoming[c].astype(f32) * et[c] + own[c].astype(f32)).astype(bf16)

        @pl.when(hops < seq - 1)
        def _():
            make(c).start()

    def chain(at):
        cf = at - lag * me
        cb = at - lag * back

        @pl.when((cf >= 0) & (cf < groups))
        def _():
            advance(cf, me, forward, s_all, p_all)

        @pl.when((cb >= 0) & (cb < groups))
        def _():
            advance(cb, back, backward, u_all, q_all)

    @pl.when(step == 0)
    def _():
        barrier = pltpu.get_barrier_semaphore()
        targets = [member(o)[1] for o in range(1, members)]
        for o in range(1, heads):
            other = lax.rem(hd + o, heads)
            targets.append({"head": other})
            targets.append({"head": other, "seq": lax.rem(me + 1, seq)})
            targets.append({"head": other, "seq": lax.rem(me + seq - 1, seq)})
        for target in targets:
            pl.semaphore_signal(barrier, inc=1, device_id=target, device_id_type=MESH)
        pl.semaphore_wait(barrier, len(targets))

        @pl.when(me < seq - 1)
        def _():
            halo_bc().start()
            halo_x().start()

        @pl.when(me == 0)
        def _():
            halo_b[...] = jnp.zeros(halo_b.shape, bf16)
            halo[...] = jnp.zeros(halo.shape, bf16)

    @pl.when(step < groups)
    def _():
        c = step
        d = d_ref[0]
        la = jnp.log(d)
        upto = (
            lax.broadcasted_iota(jnp.int32, (tokens, tokens), 0)
            <= lax.broadcasted_iota(jnp.int32, (tokens, tokens), 1)
        ).astype(f32).astype(bf16)
        rest = la
        rows = jnp.zeros(la.shape, f32)
        turned = jnp.zeros((tokens, width), f32)
        for _ in range(3):
            piece = rest.astype(bf16)
            rest = rest - piece.astype(f32)
            rows = rows + dot(piece, upto, 1, 0)
            turned = turned + dot(upto, piece, 0, 1)
        cum_r[c] = rows
        cum_t[c] = turned
        last = rows[:, tokens - 1 :]
        factors = jnp.concatenate(
            [jnp.sqrt((1.0 - d) * (1.0 + d)), jnp.exp(rows), jnp.exp(last - rows)], axis=1
        )
        high = factors.astype(bf16).astype(f32)
        both = jnp.concatenate([high, factors - high], axis=0).astype(bf16)
        fac[c] = both
        spread = dot(both, expander(width, columns, head_dim), 0, 0)
        et[c] = spread[2 * tokens - 1 : 2 * tokens]

        @pl.when(step == 0)
        def _():
            @pl.when(me > 0)
            def _():
                halo_bc().wait_recv()

            bp[0:16, :] = halo_b[...].astype(f32)
            bp[16:, :] = bc_ref[...].astype(f32)
            value, slope = silu_parts(conv_taps(bp, cbc_ref[...], first, tokens))
            mapped[...] = value.astype(bf16)
            dsbc[...] = slope

            @pl.when(me > 0)
            def _():
                halo_x().wait_recv()

        lanes = pl.ds(pl.multiple_of(c * columns, columns), columns)
        xp[0:16, :] = halo[:, lanes].astype(f32)
        xp[16:, :] = x_ref[...].astype(f32)
        value, slope = silu_parts(conv_taps(xp, cw_ref[...], first, tokens))
        inner = value.astype(bf16)
        in_all[c] = inner
        ds_all[c] = slope.astype(bf16)
        w = (inner.astype(f32) * spread[:tokens]).astype(bf16)
        w_all[c] = w
        lead = (g_ref[...].astype(f32) * spread[tokens : 2 * tokens]).astype(bf16)
        tail = (w.astype(f32) * spread[2 * tokens :]).astype(bf16)
        s_all[c] = dot(mapped[:, :n], tail, 0, 0).astype(bf16)
        u_all[c] = dot(mapped[:, n:], lead, 0, 0).astype(bf16)

    @pl.when(step < 2 * groups)
    def _():
        chain(step)

    @pl.when((step >= groups) & (step < 2 * groups))
    def _():
        c = step - groups

        @pl.when(c == 0)
        def _():
            sim[...] = dot(mapped[:, n:], mapped[:, :n], 1, 1)
            dsim[...] = jnp.zeros_like(dsim)
            dbc[...] = jnp.zeros_like(dbc)

        lower = lax.broadcasted_iota(jnp.int32, (tokens, tokens), 0) >= lax.broadcasted_iota(
            jnp.int32, (tokens, tokens), 1
        )
        pair = 2 * head_dim
        side = lax.broadcasted_iota(jnp.int32, (1, pair), 1) < head_dim
        for j in range(width // 2):
            cols = slice(j * pair, (j + 1) * pair)
            w_pair = w_all[c, :, cols]
            g_pair = g_ref[:, cols]
            parts = []
            for e in range(2):
                h = 2 * j + e
                diff = cum_t[c, :, h : h + 1] - cum_r[c, h : h + 1, :]
                decay = jnp.exp(jnp.where(lower, diff, -1e30))
                mix = (decay * sim[...]).astype(bf16)
                mine = side if e == 0 else jnp.logical_not(side)
                g_own = jnp.where(mine, g_pair.astype(f32), 0.0).astype(bf16)
                dsim[...] += decay * dot(g_own, w_pair, 1, 1)
                parts.append((dot(mix, w_pair, 1, 0), dot(mix, g_pair, 0, 0)))
            ya[c, :, cols] = jnp.where(side, parts[0][0], parts[1][0])
            da[c, :, cols] = jnp.where(side, parts[0][1], parts[1][1])

    @pl.when(step == 2 * groups)
    def _():
        for at in range(2 * groups, groups + lag * (seq - 1)):
            chain(at)

    @pl.when(step >= 2 * groups)
    def _():
        c = step - 2 * groups
        b_mat = mapped[:, :n]
        c_mat = mapped[:, n:]
        spread = dot(fac[c], expander(width, columns, head_dim), 0, 0)
        gain = spread[:tokens]
        lead = spread[tokens : 2 * tokens]
        tail = spread[2 * tokens :]
        g = g_ref[...].astype(f32)
        inner = in_all[c].astype(f32)
        p = p_all[c]
        q = q_all[c]
        y = scale * (ya[c] + lead * dot(c_mat, p, 1, 0)) + skip_ref[...] * inner
        y_ref[...] = y.astype(bf16)
        d_w = scale * (da[c] + tail * dot(b_mat, q, 1, 0))
        d_pre = (gain * d_w + skip_ref[...] * g) * ds_all[c].astype(f32)
        dbc[:, :n] += dot((w_all[c].astype(f32) * tail).astype(bf16), q, 1, 1)
        dbc[:, n:] += dot((g * lead).astype(bf16), p, 1, 1)

        lanes = pl.ds(pl.multiple_of(c * columns, columns), columns)
        xp[0:16, :] = halo[:, lanes].astype(f32)
        xp[16:, :] = x_ref[...].astype(f32)
        dp[0:tokens, :] = d_pre
        dp[tokens:, :] = jnp.zeros((8, columns), f32)
        total = jnp.zeros((tokens, columns), f32)
        for k in range(taps):
            total = total + cw_ref[k : k + 1, :] * dp[pl.ds(taps - 1 - k, tokens), :]
            parts_x[c, k : k + 1, :] = jnp.sum(
                d_pre * xp[pl.ds(first + k, tokens), :], axis=0, keepdims=True
            )
        gx_ref[:, lanes] = total.astype(bf16)
        tails[c] = total[tokens - 16 :]
        parts_x[c, taps : taps + 1, :] = jnp.sum(g * inner, axis=0, keepdims=True)
        parts_x[c, taps + 1 :, :] = jnp.zeros((8 - taps - 1, columns), f32)
        edges[c] = d_pre[0:8]

        @pl.when(me > 0)
        def _():
            edge_copy(c).start()

        @pl.when(place != lax.rem(c, members))
        def _():
            rs_copy(c).start()

    @pl.when(step == 3 * groups - 1)
    def _():
        d_sim = dsim[...].astype(bf16)
        d_b = dbc[:, :n] + dot(d_sim, mapped[:, n:], 0, 0)
        d_c = dbc[:, n:] + dot(d_sim, mapped[:, :n], 1, 0)
        dbc_out[:, :n] = (scale * d_b * dsbc[:, :n]).astype(bf16)
        dbc_out[:, n:] = (scale * d_c * dsbc[:, n:]).astype(bf16)
        for o in range(1, heads):
            head_copy(o).start()

        @pl.when(me > 0)
        def _():
            for o in range(heads):
                nbc_copy(o).start()

        head_in[hd] = dbc_out[...]
        for c in range(groups):
            @pl.when(place == c % members)
            def _():
                for o in range(1, members):
                    at = lax.rem(place + o, members)
                    arrived(rs_in.at[c, at], rs_recv.at[c, at], parts_x.at[c])
                rs_in[c, c % members] = parts_x[c]
                total = rs_in[c, 0]
                for i in range(1, members):
                    total = total + rs_in[c, i]
                ag_in[c] = total
                for o in range(1, members):
                    ag_copy(c, o).start()

        for o in range(1, heads):
            at = lax.rem(hd + o, heads)
            arrived(head_in.at[at], head_recv.at[at], dbc_out)
        full = head_in[0].astype(f32)
        for h in range(1, heads):
            full = full + head_in[h].astype(f32)
        for k in range(taps):
            bct[k : k + 1, :] = jnp.sum(
                full * bp[pl.ds(first + k, tokens), :], axis=0, keepdims=True
            )
        bct[taps:, :] = jnp.zeros((8 - taps, bct.shape[1]), f32)
        for o in range(1, members):
            bct_copy(o).start()
        bct_in[place] = bct[...]
        dbp[0:tokens, :] = full

        @pl.when(me == seq - 1)
        def _():
            dbp[tokens:, :] = jnp.zeros((8, full.shape[1]), f32)

        @pl.when(me < seq - 1)
        def _():
            at = lax.broadcasted_iota(jnp.int32, (16, 1), 0)
            for c in range(groups):
                edge_copy(c).wait_recv()
                cols = slice(c * columns, (c + 1) * columns)
                fixed = tails[c]
                for r in range(taps - 1):
                    row = jnp.zeros((1, columns), f32)
                    for k in range(r + 1):
                        row = row + cw_all_ref[k : k + 1, cols] * next_x[c, r - k : r - k + 1, :]
                    fixed = fixed + jnp.where(at == 16 - (taps - 1) + r, row, 0.0)
                gx_ref[tokens - 16 :, cols] = fixed.astype(bf16)
            for o in range(heads):
                arrived(next_bc.at[o], nbc_recv.at[o], dbc_out.at[0:16])
            rows = next_bc[0].astype(f32)
            for h in range(1, heads):
                rows = rows + next_bc[h].astype(f32)
            dbp[tokens:, :] = rows[0:8]

        grad = jnp.zeros(full.shape, f32)
        for k in range(taps):
            grad = grad + cbc_ref[k : k + 1, :] * dbp[pl.ds(taps - 1 - k, tokens), :]
        gbc_ref[...] = grad.astype(bf16)

        for c in range(groups):
            @pl.when(place != c % members)
            def _():
                arrived(ag_in.at[c], ag_recv.at[c], ag_in.at[c])
            cols = slice(c * columns, (c + 1) * columns)
            sums_ref[:, cols] = ag_in[c, 0:taps] * norm
            skips_ref[:, cols] = ag_in[c, taps : taps + 1] * norm
        for o in range(1, members):
            at = lax.rem(place + o, members)
            arrived(bct_in.at[at], bct_recv.at[at], bct)
        bsum = bct_in[0]
        for i in range(1, members):
            bsum = bsum + bct_in[i]
        bsum_ref[...] = bsum[0:taps] * norm

        for o in range(1, heads):
            head_copy(o).wait_send()
        for o in range(1, members):
            bct_copy(o).wait_send()
        for c in range(groups):
            @pl.when(place == c % members)
            def _():
                for o in range(1, members):
                    ag_copy(c, o).wait_send()

            @pl.when(place != c % members)
            def _():
                rs_copy(c).wait_send()

        @pl.when(me > 0)
        def _():
            for o in range(heads):
                nbc_copy(o).wait_send()
            for c in range(groups):
                edge_copy(c).wait_send()

        @pl.when(me < seq - 1)
        def _():
            halo_bc().wait_send()
            halo_x().wait_send()

        @pl.loop(0, groups)
        def _(c):
            @pl.when(me < seq - 1)
            def _():
                forward(c).wait_send()

            @pl.when(me > 0)
            def _():
                backward(c).wait_send()


def local(x_input, bc_input, decays, conv_x, conv_bc, skip_gain, grad_out):
    x = x_input[0]
    bc = bc_input[0]
    d = decays[0]
    g = grad_out[0]
    tokens, channels = x.shape
    taps = conv_x.shape[0]
    heads = d.shape[0]
    head_dim = channels // heads
    n = bc.shape[1] // 2
    scale = float(n) ** (-0.5)
    seq = lax.axis_size("seq")
    width = next(k for k in (8, 4, 2) if heads % k == 0)
    groups = heads // width
    columns = width * head_dim

    decay_rows = d.reshape(groups, width, tokens)
    skip = jnp.repeat(skip_gain, head_dim)[None, :]

    def cols(rows):
        return pl.BlockSpec((rows, columns), lambda i: (0, lax.rem(i, groups)))

    def late(rows):
        return pl.BlockSpec((rows, columns), lambda i: (0, lax.max(i - 2 * groups, 0)))

    def whole(rows, c, at=0):
        return pl.BlockSpec((rows, c), lambda i: (at, 0))

    def out(shape, dtype):
        return jax.ShapeDtypeStruct(shape, dtype)

    dma = pltpu.SemaphoreType.DMA
    wide = (groups, tokens, columns)
    head_devices = lax.axis_size("head")
    cores = lax.axis_size("dp")
    members = seq * cores
    norm = float(tokens * members) ** (-0.5)
    sizes = (seq, head_devices, cores)
    block = (groups, 8, columns)
    y, gx, gbc, sums, skips, taps_bc = pl.pallas_call(
        functools.partial(main_kernel, head_dim, scale, norm, sizes, 2),
        grid=(3 * groups,),
        in_specs=[
            cols(tokens), whole(16, channels, tokens // 16 - 1), whole(tokens, 2 * n),
            whole(16, 2 * n, tokens // 16 - 1),
            pl.BlockSpec((1, width, tokens), lambda i: (lax.rem(i, groups), 0, 0)),
            cols(taps), whole(taps, channels), whole(taps, 2 * n), cols(1), cols(tokens),
        ],
        out_specs=[
            late(tokens), whole(tokens, channels), whole(tokens, 2 * n), whole(taps, channels),
            whole(1, channels), whole(taps, 2 * n),
        ],
        out_shape=[
            out((tokens, channels), bf16), out((tokens, channels), bf16),
            out((tokens, 2 * n), bf16), out((taps, channels), f32), out((1, channels), f32),
            out((taps, 2 * n), f32),
        ],
        scratch_shapes=[
            pltpu.VMEM(wide, bf16), pltpu.VMEM(wide, bf16), pltpu.VMEM(wide, bf16),
            pltpu.VMEM(wide, f32), pltpu.VMEM(wide, f32),
            pltpu.VMEM((groups, n, columns), bf16), pltpu.VMEM((groups, n, columns), bf16),
            pltpu.VMEM((groups, n, columns), bf16), pltpu.VMEM((groups, n, columns), bf16),
            pltpu.VMEM((groups, 1, columns), f32), pltpu.VMEM((groups, 2 * width, 3 * tokens), bf16),
            pltpu.VMEM((groups, width, tokens), f32), pltpu.VMEM((groups, tokens, width), f32),
            pltpu.VMEM((16, channels), bf16), pltpu.VMEM((16, 2 * n), bf16),
            pltpu.VMEM((tokens, 2 * n), bf16),
            pltpu.VMEM((tokens, 2 * n), f32), pltpu.VMEM((tokens + 16, 2 * n), f32),
            pltpu.VMEM((tokens + 16, columns), f32), pltpu.VMEM((tokens + 8, columns), f32),
            pltpu.VMEM((tokens, tokens), f32), pltpu.VMEM((tokens, tokens), f32),
            pltpu.VMEM((tokens, 2 * n), f32),
            pltpu.VMEM((groups, 16, columns), f32), pltpu.VMEM(block, f32),
            pltpu.VMEM(block, f32), pltpu.VMEM(block, f32),
            pltpu.VMEM((groups, members, 8, columns), f32), pltpu.VMEM(block, f32),
            pltpu.VMEM((8, 2 * n), f32), pltpu.VMEM((members, 8, 2 * n), f32),
            pltpu.VMEM((tokens, 2 * n), bf16), pltpu.VMEM((head_devices, tokens, 2 * n), bf16),
            pltpu.VMEM((head_devices, 16, 2 * n), bf16), pltpu.VMEM((tokens + 8, 2 * n), f32),
            dma((2,)), dma((2,)),
            dma((groups,)), dma((groups,)), dma((groups,)), dma((groups,)),
            dma((groups,)), dma((groups,)), dma((groups,)), dma((groups, members)),
            dma((groups, members)), dma((groups,)), dma((members,)), dma((members,)),
            dma((head_devices,)), dma((head_devices,)), dma((head_devices,)),
            dma((head_devices,)),
        ],
        compiler_params=pltpu.CompilerParams(
            dimension_semantics=("arbitrary",), vmem_limit_bytes=60 * 1024 * 1024,
            collective_id=0, has_side_effects=True,
        ),
        name="main",
    )(x, x, bc, bc, decay_rows, conv_x, conv_x, conv_bc, skip, g)

    skip_sum = jnp.sum(skips.reshape(heads, head_dim), axis=1)
    return (
        y[None],
        gx[None],
        gbc[None],
        sums,
        taps_bc,
        skip_sum * float(head_dim) ** (-0.5),
    )


def solution(mesh):
    return jax.shard_map(
        local,
        mesh=mesh,
        in_specs=(
            P(("groups", "dp"), "seq", "head"),
            P(("groups", "dp"), "seq", None),
            P(("groups", "dp"), "head", "seq"),
            P(None, "head"),
            P(),
            P("head"),
            P(("groups", "dp"), "seq", "head"),
        ),
        out_specs=(
            P(("groups", "dp"), "seq", "head"),
            P(("groups", "dp"), "seq", "head"),
            P(("groups", "dp"), "seq", None),
            P("groups", "head"),
            P("groups", None),
            P(("groups", "head")),
        ),
        check_vma=False,
    )
```

```python
import functools

import jax
import jax.numpy as jnp
from jax import lax
from jax.experimental import pallas as pl
from jax.experimental.pallas import tpu as pltpu
from jax.sharding import PartitionSpec as P

MESH = pl.DeviceIdType.MESH
f32 = jnp.float32
bf16 = jnp.bfloat16


def dot(a, b, ca, cb):
    return lax.dot_general(a, b, (((ca,), (cb,)), ((), ())), preferred_element_type=f32)


def expander(width, columns, head_dim):
    rows = lax.broadcasted_iota(jnp.int32, (2 * width, columns), 0) % width
    cols = lax.broadcasted_iota(jnp.int32, (2 * width, columns), 1) // head_dim
    return (rows == cols).astype(f32).astype(bf16)


def conv_taps(pad_ref, weight, first, tokens):
    total = weight[0:1, :] * pad_ref[pl.ds(first, tokens), :]
    for k in range(1, weight.shape[0]):
        total = total + weight[k : k + 1, :] * pad_ref[pl.ds(first + k, tokens), :]
    return total


def silu_parts(pre):
    sigma = jax.nn.sigmoid(pre)
    return pre * sigma, sigma * (1.0 + pre * (1.0 - sigma))


def main_kernel(
    head_dim, scale, norm, sizes, lag, x_ref, x_end_ref, bc_ref, bc_end_ref, d_ref, cw_ref,
    cw_all_ref, cbc_ref, skip_ref, g_ref, y_ref, gx_ref, gbc_ref, sums_ref, skips_ref, bsum_ref,
    w_all, in_all, ds_all, ya, da, s_all, u_all, p_all, q_all, et, fac, cum_r, cum_t, halo, halo_b,
    mapped, dsbc, bp, xp, dp, sim, dsim, dbc,
    tails, edges, parts_x, next_x, rs_in, ag_in, bct, bct_in, dbc_out, head_in, next_bc, dbp,
    halo_send, halo_recv, send_f, recv_f, send_b, recv_b,
    edge_send, edge_recv, rs_send, rs_recv, ag_send, ag_recv, bct_send, bct_recv,
    head_send, head_recv, nbc_send, nbc_recv,
):
    step = pl.program_id(0)
    groups = w_all.shape[0]
    tokens, columns = x_ref.shape
    width = columns // head_dim
    n = mapped.shape[1] // 2
    taps = cw_ref.shape[0]
    first = 17 - taps
    seq, heads, cores = sizes
    members = seq * cores
    me = lax.axis_index("seq")
    back = seq - 1 - me
    hd = lax.axis_index("head")
    place = me * cores + lax.axis_index("dp")

    def member(offset):
        at = lax.rem(place + offset, members)
        return at, {"seq": at // cores, "dp": lax.rem(at, cores)}

    def copy(src, dst, send, recv, device):
        return pltpu.make_async_remote_copy(
            src_ref=src, dst_ref=dst, send_sem=send, recv_sem=recv, device_id=device,
            device_id_type=MESH,
        )

    def head_copy(o):
        return copy(
            dbc_out, head_in.at[hd], head_send.at[o], head_recv.at[hd],
            {"head": lax.rem(hd + o, heads)},
        )

    def nbc_copy(o):
        return copy(
            dbc_out.at[0:16], next_bc.at[hd], nbc_send.at[o], nbc_recv.at[hd],
            {"head": lax.rem(hd + o, heads), "seq": me - 1},
        )

    def edge_copy(c):
        return copy(
            edges.at[c], next_x.at[c], edge_send.at[c], edge_recv.at[c], {"seq": me - 1}
        )

    def rs_copy(c):
        owner = lax.rem(c, members)
        return copy(
            parts_x.at[c], rs_in.at[c, place], rs_send.at[c], rs_recv.at[c, place],
            {"seq": owner // cores, "dp": lax.rem(owner, cores)},
        )

    def ag_copy(c, o):
        return copy(ag_in.at[c], ag_in.at[c], ag_send.at[c, o], ag_recv.at[c], member(o)[1])

    def bct_copy(o):
        return copy(bct, bct_in.at[place], bct_send.at[o], bct_recv.at[place], member(o)[1])

    def arrived(dst, sem, source):
        copy(source, dst, sem, sem, member(1)[1]).wait_recv()

    def remote(src, dst, send, recv, distance):
        return pltpu.make_async_remote_copy(
            src_ref=src, dst_ref=dst, send_sem=send, recv_sem=recv,
            device_id={"seq": me + distance}, device_id_type=MESH,
        )

    def halo_x():
        return remote(x_end_ref, halo, halo_send.at[0], halo_recv.at[0], 1)

    def halo_bc():
        return remote(bc_end_ref, halo_b, halo_send.at[1], halo_recv.at[1], 1)

    def forward(c):
        return remote(s_all.at[c], p_all.at[c], send_f.at[c], recv_f.at[c], 1)

    def backward(c):
        return remote(u_all.at[c], q_all.at[c], send_b.at[c], recv_b.at[c], -1)

    def advance(c, hops, make, own, incoming):
        @pl.when(hops == 0)
        def _():
            incoming[c] = jnp.zeros(incoming.shape[1:], bf16)

        @pl.when(hops > 0)
        def _():
            make(c).wait_recv()

            @pl.when(hops < seq - 1)
            def _():
                own[c] = (incoming[c].astype(f32) * et[c] + own[c].astype(f32)).astype(bf16)

        @pl.when(hops < seq - 1)
        def _():
            make(c).start()

    def chain(at):
        cf = at - lag * me
        cb = at - lag * back

        @pl.when((cf >= 0) & (cf < groups))
        def _():
            advance(cf, me, forward, s_all, p_all)

        @pl.when((cb >= 0) & (cb < groups))
        def _():
            advance(cb, back, backward, u_all, q_all)

    @pl.when(step == 0)
    def _():
        barrier = pltpu.get_barrier_semaphore()
        targets = [member(o)[1] for o in range(1, members)]
        for o in range(1, heads):
            other = lax.rem(hd + o, heads)
            targets.append({"head": other})
            targets.append({"head": other, "seq": lax.rem(me + 1, seq)})
            targets.append({"head": other, "seq": lax.rem(me + seq - 1, seq)})
        for target in targets:
            pl.semaphore_signal(barrier, inc=1, device_id=target, device_id_type=MESH)
        pl.semaphore_wait(barrier, len(targets))

        @pl.when(me < seq - 1)
        def _():
            halo_bc().start()
            halo_x().start()

        @pl.when(me == 0)
        def _():
            halo_b[...] = jnp.zeros(halo_b.shape, bf16)
            halo[...] = jnp.zeros(halo.shape, bf16)

    @pl.when(step < groups)
    def _():
        c = step
        d = d_ref[0]
        la = jnp.log(d)
        upto = (
            lax.broadcasted_iota(jnp.int32, (tokens, tokens), 0)
            <= lax.broadcasted_iota(jnp.int32, (tokens, tokens), 1)
        ).astype(f32).astype(bf16)
        rest = la
        rows = jnp.zeros(la.shape, f32)
        turned = jnp.zeros((tokens, width), f32)
        for _ in range(3):
            piece = rest.astype(bf16)
            rest = rest - piece.astype(f32)
            rows = rows + dot(piece, upto, 1, 0)
            turned = turned + dot(upto, piece, 0, 1)
        cum_r[c] = rows
        cum_t[c] = turned
        last = rows[:, tokens - 1 :]
        factors = jnp.concatenate(
            [jnp.sqrt((1.0 - d) * (1.0 + d)), jnp.exp(rows), jnp.exp(last - rows)], axis=1
        )
        high = factors.astype(bf16).astype(f32)
        both = jnp.concatenate([high, factors - high], axis=0).astype(bf16)
        fac[c] = both
        spread = dot(both, expander(width, columns, head_dim), 0, 0)
        et[c] = spread[2 * tokens - 1 : 2 * tokens]

        @pl.when(step == 0)
        def _():
            @pl.when(me > 0)
            def _():
                halo_bc().wait_recv()

            bp[0:16, :] = halo_b[...].astype(f32)
            bp[16:, :] = bc_ref[...].astype(f32)
            value, slope = silu_parts(conv_taps(bp, cbc_ref[...], first, tokens))
            mapped[...] = value.astype(bf16)
            dsbc[...] = slope

            @pl.when(me > 0)
            def _():
                halo_x().wait_recv()

        lanes = pl.ds(pl.multiple_of(c * columns, columns), columns)
        xp[0:16, :] = halo[:, lanes].astype(f32)
        xp[16:, :] = x_ref[...].astype(f32)
        value, slope = silu_parts(conv_taps(xp, cw_ref[...], first, tokens))
        inner = value.astype(bf16)
        in_all[c] = inner
        ds_all[c] = slope.astype(bf16)
        w = (inner.astype(f32) * spread[:tokens]).astype(bf16)
        w_all[c] = w
        lead = (g_ref[...].astype(f32) * spread[tokens : 2 * tokens]).astype(bf16)
        tail = (w.astype(f32) * spread[2 * tokens :]).astype(bf16)
        s_all[c] = dot(mapped[:, :n], tail, 0, 0).astype(bf16)
        u_all[c] = dot(mapped[:, n:], lead, 0, 0).astype(bf16)

    @pl.when(step < 2 * groups)
    def _():
        chain(step)

    @pl.when((step >= groups) & (step < 2 * groups))
    def _():
        c = step - groups

        @pl.when(c == 0)
        def _():
            sim[...] = dot(mapped[:, n:], mapped[:, :n], 1, 1)
            dsim[...] = jnp.zeros_like(dsim)
            dbc[...] = jnp.zeros_like(dbc)

        lower = lax.broadcasted_iota(jnp.int32, (tokens, tokens), 0) >= lax.broadcasted_iota(
            jnp.int32, (tokens, tokens), 1
        )
        pair = 2 * head_dim
        side = lax.broadcasted_iota(jnp.int32, (1, pair), 1) < head_dim
        for j in range(width // 2):
            cols = slice(j * pair, (j + 1) * pair)
            w_pair = w_all[c, :, cols]
            g_pair = g_ref[:, cols]
            parts = []
            for e in range(2):
                h = 2 * j + e
                diff = cum_t[c, :, h : h + 1] - cum_r[c, h : h + 1, :]
                decay = jnp.exp(jnp.where(lower, diff, -1e30))
                mix = (decay * sim[...]).astype(bf16)
                mine = side if e == 0 else jnp.logical_not(side)
                g_own = jnp.where(mine, g_pair.astype(f32), 0.0).astype(bf16)
                dsim[...] += decay * dot(g_own, w_pair, 1, 1)
                parts.append((dot(mix, w_pair, 1, 0), dot(mix, g_pair, 0, 0)))
            ya[c, :, cols] = jnp.where(side, parts[0][0], parts[1][0])
            da[c, :, cols] = jnp.where(side, parts[0][1], parts[1][1])

    @pl.when(step == 2 * groups)
    def _():
        for at in range(2 * groups, groups + lag * (seq - 1)):
            chain(at)

    @pl.when(step >= 2 * groups)
    def _():
        c = step - 2 * groups
        b_mat = mapped[:, :n]
        c_mat = mapped[:, n:]
        spread = dot(fac[c], expander(width, columns, head_dim), 0, 0)
        gain = spread[:tokens]
        lead = spread[tokens : 2 * tokens]
        tail = spread[2 * tokens :]
        g = g_ref[...].astype(f32)
        inner = in_all[c].astype(f32)
        lane = lax.broadcasted_iota(jnp.int32, (1, columns), 1) // head_dim
        skip = jnp.zeros((1, columns), f32)
        for j in range(width):
            skip = jnp.where(lane == j, skip_ref[c * width + j], skip)
        p = p_all[c]
        q = q_all[c]
        y = scale * (ya[c] + lead * dot(c_mat, p, 1, 0)) + skip * inner
        y_ref[...] = y.astype(bf16)
        d_w = scale * (da[c] + tail * dot(b_mat, q, 1, 0))
        d_pre = (gain * d_w + skip * g) * ds_all[c].astype(f32)
        dbc[:, :n] += dot((w_all[c].astype(f32) * tail).astype(bf16), q, 1, 1)
        dbc[:, n:] += dot((g * lead).astype(bf16), p, 1, 1)

        lanes = pl.ds(pl.multiple_of(c * columns, columns), columns)
        xp[0:16, :] = halo[:, lanes].astype(f32)
        xp[16:, :] = x_ref[...].astype(f32)
        dp[0:tokens, :] = d_pre
        dp[tokens:, :] = jnp.zeros((8, columns), f32)
        total = jnp.zeros((tokens, columns), f32)
        for k in range(taps):
            total = total + cw_ref[k : k + 1, :] * dp[pl.ds(taps - 1 - k, tokens), :]
            parts_x[c, k : k + 1, :] = jnp.sum(
                d_pre * xp[pl.ds(first + k, tokens), :], axis=0, keepdims=True
            )
        gx_ref[:, lanes] = total.astype(bf16)
        tails[c] = total[tokens - 16 :]
        parts_x[c, taps : taps + 1, :] = jnp.sum(g * inner, axis=0, keepdims=True)
        parts_x[c, taps + 1 :, :] = jnp.zeros((8 - taps - 1, columns), f32)
        edges[c] = d_pre[0:8]

        @pl.when(me > 0)
        def _():
            edge_copy(c).start()

        @pl.when(place != lax.rem(c, members))
        def _():
            rs_copy(c).start()

    @pl.when(step == 3 * groups - 1)
    def _():
        d_sim = dsim[...].astype(bf16)
        d_b = dbc[:, :n] + dot(d_sim, mapped[:, n:], 0, 0)
        d_c = dbc[:, n:] + dot(d_sim, mapped[:, :n], 1, 0)
        dbc_out[:, :n] = (scale * d_b * dsbc[:, :n]).astype(bf16)
        dbc_out[:, n:] = (scale * d_c * dsbc[:, n:]).astype(bf16)
        for o in range(1, heads):
            head_copy(o).start()

        @pl.when(me > 0)
        def _():
            for o in range(heads):
                nbc_copy(o).start()

        head_in[hd] = dbc_out[...]
        for c in range(groups):
            @pl.when(place == c % members)
            def _():
                for o in range(1, members):
                    at = lax.rem(place + o, members)
                    arrived(rs_in.at[c, at], rs_recv.at[c, at], parts_x.at[c])
                rs_in[c, c % members] = parts_x[c]
                total = rs_in[c, 0]
                for i in range(1, members):
                    total = total + rs_in[c, i]
                ag_in[c] = total
                for o in range(1, members):
                    ag_copy(c, o).start()

        for o in range(1, heads):
            at = lax.rem(hd + o, heads)
            arrived(head_in.at[at], head_recv.at[at], dbc_out)
        full = head_in[0].astype(f32)
        for h in range(1, heads):
            full = full + head_in[h].astype(f32)
        for k in range(taps):
            bct[k : k + 1, :] = jnp.sum(
                full * bp[pl.ds(first + k, tokens), :], axis=0, keepdims=True
            )
        bct[taps:, :] = jnp.zeros((8 - taps, bct.shape[1]), f32)
        for o in range(1, members):
            bct_copy(o).start()
        bct_in[place] = bct[...]
        dbp[0:tokens, :] = full

        @pl.when(me == seq - 1)
        def _():
            dbp[tokens:, :] = jnp.zeros((8, full.shape[1]), f32)

        @pl.when(me < seq - 1)
        def _():
            at = lax.broadcasted_iota(jnp.int32, (16, 1), 0)
            for c in range(groups):
                edge_copy(c).wait_recv()
                cols = slice(c * columns, (c + 1) * columns)
                fixed = tails[c]
                for r in range(taps - 1):
                    row = jnp.zeros((1, columns), f32)
                    for k in range(r + 1):
                        row = row + cw_all_ref[k : k + 1, cols] * next_x[c, r - k : r - k + 1, :]
                    fixed = fixed + jnp.where(at == 16 - (taps - 1) + r, row, 0.0)
                gx_ref[tokens - 16 :, cols] = fixed.astype(bf16)
            for o in range(heads):
                arrived(next_bc.at[o], nbc_recv.at[o], dbc_out.at[0:16])
            rows = next_bc[0].astype(f32)
            for h in range(1, heads):
                rows = rows + next_bc[h].astype(f32)
            dbp[tokens:, :] = rows[0:8]

        grad = jnp.zeros(full.shape, f32)
        for k in range(taps):
            grad = grad + cbc_ref[k : k + 1, :] * dbp[pl.ds(taps - 1 - k, tokens), :]
        gbc_ref[...] = grad.astype(bf16)

        for c in range(groups):
            @pl.when(place != c % members)
            def _():
                arrived(ag_in.at[c], ag_recv.at[c], ag_in.at[c])
            cols = slice(c * columns, (c + 1) * columns)
            sums_ref[:, cols] = ag_in[c, 0:taps] * norm
            skips_ref[:, cols] = ag_in[c, taps : taps + 1] * norm
        for o in range(1, members):
            at = lax.rem(place + o, members)
            arrived(bct_in.at[at], bct_recv.at[at], bct)
        bsum = bct_in[0]
        for i in range(1, members):
            bsum = bsum + bct_in[i]
        bsum_ref[...] = bsum[0:taps] * norm

        for o in range(1, heads):
            head_copy(o).wait_send()
        for o in range(1, members):
            bct_copy(o).wait_send()
        for c in range(groups):
            @pl.when(place == c % members)
            def _():
                for o in range(1, members):
                    ag_copy(c, o).wait_send()

            @pl.when(place != c % members)
            def _():
                rs_copy(c).wait_send()

        @pl.when(me > 0)
        def _():
            for o in range(heads):
                nbc_copy(o).wait_send()
            for c in range(groups):
                edge_copy(c).wait_send()

        @pl.when(me < seq - 1)
        def _():
            halo_bc().wait_send()
            halo_x().wait_send()

        @pl.loop(0, groups)
        def _(c):
            @pl.when(me < seq - 1)
            def _():
                forward(c).wait_send()

            @pl.when(me > 0)
            def _():
                backward(c).wait_send()


def local(x_input, bc_input, decays, conv_x, conv_bc, skip_gain, grad_out):
    x = x_input[0]
    bc = bc_input[0]
    d = decays[0]
    g = grad_out[0]
    tokens, channels = x.shape
    taps = conv_x.shape[0]
    heads = d.shape[0]
    head_dim = channels // heads
    n = bc.shape[1] // 2
    scale = float(n) ** (-0.5)
    seq = lax.axis_size("seq")
    width = next(k for k in (8, 4, 2) if heads % k == 0)
    groups = heads // width
    columns = width * head_dim

    decay_rows = d.reshape(groups, width, tokens)

    def cols(rows):
        return pl.BlockSpec((rows, columns), lambda i: (0, lax.rem(i, groups)))

    def late(rows):
        return pl.BlockSpec((rows, columns), lambda i: (0, lax.max(i - 2 * groups, 0)))

    def whole(rows, c, at=0):
        return pl.BlockSpec((rows, c), lambda i: (at, 0))

    def out(shape, dtype):
        return jax.ShapeDtypeStruct(shape, dtype)

    dma = pltpu.SemaphoreType.DMA
    wide = (groups, tokens, columns)
    head_devices = lax.axis_size("head")
    cores = lax.axis_size("dp")
    members = seq * cores
    norm = float(tokens * members) ** (-0.5)
    sizes = (seq, head_devices, cores)
    block = (groups, 8, columns)
    y, gx, gbc, sums, skips, taps_bc = pl.pallas_call(
        functools.partial(main_kernel, head_dim, scale, norm, sizes, 2),
        grid=(3 * groups,),
        in_specs=[
            cols(tokens), whole(16, channels, tokens // 16 - 1), whole(tokens, 2 * n),
            whole(16, 2 * n, tokens // 16 - 1),
            pl.BlockSpec((1, width, tokens), lambda i: (lax.rem(i, groups), 0, 0)),
            cols(taps), whole(taps, channels), whole(taps, 2 * n),
            pl.BlockSpec(memory_space=pltpu.SMEM), cols(tokens),
        ],
        out_specs=[
            late(tokens), whole(tokens, channels), whole(tokens, 2 * n), whole(taps, channels),
            whole(1, channels), whole(taps, 2 * n),
        ],
        out_shape=[
            out((tokens, channels), bf16), out((tokens, channels), bf16),
            out((tokens, 2 * n), bf16), out((taps, channels), f32), out((1, channels), f32),
            out((taps, 2 * n), f32),
        ],
        scratch_shapes=[
            pltpu.VMEM(wide, bf16), pltpu.VMEM(wide, bf16), pltpu.VMEM(wide, bf16),
            pltpu.VMEM(wide, f32), pltpu.VMEM(wide, f32),
            pltpu.VMEM((groups, n, columns), bf16), pltpu.VMEM((groups, n, columns), bf16),
            pltpu.VMEM((groups, n, columns), bf16), pltpu.VMEM((groups, n, columns), bf16),
            pltpu.VMEM((groups, 1, columns), f32), pltpu.VMEM((groups, 2 * width, 3 * tokens), bf16),
            pltpu.VMEM((groups, width, tokens), f32), pltpu.VMEM((groups, tokens, width), f32),
            pltpu.VMEM((16, channels), bf16), pltpu.VMEM((16, 2 * n), bf16),
            pltpu.VMEM((tokens, 2 * n), bf16),
            pltpu.VMEM((tokens, 2 * n), f32), pltpu.VMEM((tokens + 16, 2 * n), f32),
            pltpu.VMEM((tokens + 16, columns), f32), pltpu.VMEM((tokens + 8, columns), f32),
            pltpu.VMEM((tokens, tokens), f32), pltpu.VMEM((tokens, tokens), f32),
            pltpu.VMEM((tokens, 2 * n), f32),
            pltpu.VMEM((groups, 16, columns), f32), pltpu.VMEM(block, f32),
            pltpu.VMEM(block, f32), pltpu.VMEM(block, f32),
            pltpu.VMEM((groups, members, 8, columns), f32), pltpu.VMEM(block, f32),
            pltpu.VMEM((8, 2 * n), f32), pltpu.VMEM((members, 8, 2 * n), f32),
            pltpu.VMEM((tokens, 2 * n), bf16), pltpu.VMEM((head_devices, tokens, 2 * n), bf16),
            pltpu.VMEM((head_devices, 16, 2 * n), bf16), pltpu.VMEM((tokens + 8, 2 * n), f32),
            dma((2,)), dma((2,)),
            dma((groups,)), dma((groups,)), dma((groups,)), dma((groups,)),
            dma((groups,)), dma((groups,)), dma((groups,)), dma((groups, members)),
            dma((groups, members)), dma((groups,)), dma((members,)), dma((members,)),
            dma((head_devices,)), dma((head_devices,)), dma((head_devices,)),
            dma((head_devices,)),
        ],
        compiler_params=pltpu.CompilerParams(
            dimension_semantics=("arbitrary",), vmem_limit_bytes=60 * 1024 * 1024,
            collective_id=0, has_side_effects=True,
        ),
        name="main",
    )(x, x, bc, bc, decay_rows, conv_x, conv_x, conv_bc, skip_gain, g)

    skip_sum = jnp.sum(skips.reshape(heads, head_dim), axis=1)
    return (
        y[None],
        gx[None],
        gbc[None],
        sums,
        taps_bc,
        skip_sum * float(head_dim) ** (-0.5),
    )


def solution(mesh):
    return jax.shard_map(
        local,
        mesh=mesh,
        in_specs=(
            P(("groups", "dp"), "seq", "head"),
            P(("groups", "dp"), "seq", None),
            P(("groups", "dp"), "head", "seq"),
            P(None, "head"),
            P(),
            P("head"),
            P(("groups", "dp"), "seq", "head"),
        ),
        out_specs=(
            P(("groups", "dp"), "seq", "head"),
            P(("groups", "dp"), "seq", "head"),
            P(("groups", "dp"), "seq", None),
            P("groups", "head"),
            P("groups", None),
            P(("groups", "head")),
        ),
        check_vma=False,
    )
```
